32 devices in a mesh: group: 1, expert: 16 (over z, y, x), dp: 2 (over core).
Axes of the slice: x: 2, y: 2, z: 4, core: 2. Of those that a mesh axis runs over, the one named last changes fastest.
Arguments:
- tokens: bfloat16 [2048, 4096], P(('group', 'expert', 'dp')), may hold values from -6 to 6
- queries: bfloat16 [2048, 4096], P(('group', 'expert', 'dp')), may hold values from -6 to 6
- keys_local: bfloat16 [2048, 256], P(('group', 'expert', 'dp')), may hold values from -6 to 6
- values_local: bfloat16 [2048, 256], P(('group', 'expert', 'dp')), may hold values from -6 to 6
- prompt_keys: bfloat16 [1024, 256], P('group'), may hold values from -6 to 6
- prompt_values: bfloat16 [1024, 256], P('group'), may hold values from -6 to 6
- norm_gain: float32 [4096], replicated, may hold values from 0.25 to 1.75
- expert_ids: int32 [2048, 8], P(('group', 'expert', 'dp')), may hold values from 0 to 15, all different within a row; in each aligned block of 64 rows (0 to 63, 64 to 127, ...) at most 42 rows name the same one
- route_weight: float32 [2048, 8], P(('group', 'expert', 'dp')), may hold values from 0.05 to 1
- stored_gate: bfloat16 [16, 4096, 768], P('expert', None, 'dp'), may hold values from -0.09375 to 0.09375
- stored_up: bfloat16 [16, 4096, 768], P('expert', None, 'dp'), may hold values from -0.09375 to 0.09375
- stored_down: bfloat16 [16, 768, 4096], P('expert', 'dp'), may hold values from -0.21875 to 0.21875
- holder: int32 [16], replicated, may hold values from 0 to 15, as said below
Outputs:
- layer_out: bfloat16 [2048, 4096], P(('group', 'expert', 'dp'))
The draws below stay inside these ranges and needn't reach their ends.
Inputs may be any that keep to these rules, and one draw needn't show every extreme that they name: `expert_ids`: each row names 8 different experts. In the 64 rows of one device no expert is named more than 42 times, and in every draw some expert is named exactly 42 times in some device's rows. holder[s] is s or the slot 8 away (s + 16 / 2 modulo 16), holder[holder[s]] = s, and holder[0] = 8.
All inputs are finite; a program needn't handle non-finite values.
Results may differ from the reference program's by a relative error of at most 0.0055.
Values may be sent and summed in bfloat16 or wider, within the bound.
No kernel may reach another device: no remote copies, remote signals or barrier semaphores. Data moves between devices by JAX's collectives and lax.ppermute only.
A program may use at most 192 MiB of HBM per device.

```python
import math
import jax
import jax.numpy as jnp
import numpy as np
from jax import lax

D = 4096
FFW = 768
HEADS = 32
KVH = 2
HD = 128
TOPK = 8
PREFIX = 1024
TOK_DEV = 64
EXPERTS = 16
SPLITS = 2
CAP = 42
TOKENS = 2048


def drawn_keys(key):
    base = jax.random.fold_in(key, 11)
    key_width = KVH * HD
    drawn = jnp.clip(jax.random.normal(jax.random.fold_in(base, 3), (PREFIX, key_width), jnp.float32), -5.5, 5.5)
    return drawn


def draw_prompt_keys(key, part):
    drawn = drawn_keys(key)
    return drawn.astype(jnp.bfloat16)


def draw_queries(key, part):
    base = jax.random.fold_in(key, 23)
    values = jnp.clip(jax.random.normal(base, (TOKENS, HEADS * HD), jnp.float32), -5.5, 5.5)
    return values.astype(jnp.bfloat16)


def draw_holder(key, part):
    half_count = EXPERTS // 2
    flags = jax.random.randint(jax.random.fold_in(key, 3), (half_count,), 0, 2)
    flags = flags.at[0].set(1)
    lower_half = jnp.arange(half_count) + flags * half_count
    upper_half = jnp.arange(half_count) + half_count - flags * half_count
    return jnp.concatenate([lower_half, upper_half]).astype(jnp.int32)


def steps_of(stream_key, dims, shards, smallest, top_value):
    level, own = 1.0, jax.random.fold_in(stream_key, 6)
    for dim, parts in shards:
        steps = jnp.exp(jax.random.uniform(jax.random.fold_in(own, dim), (parts,), jnp.float32, smallest / len(shards), top_value / len(shards)))
        level = level * jnp.repeat(steps, dims[dim] // parts).reshape([-1 if axis == dim else 1 for axis in range(len(dims))])
    return level


def routed_block(key, own, number, rows, number_of, top, most, skew):
    order = jax.random.permutation(key, number_of)
    packed, usual = load_shares(number_of, rows * top, most, skew, True), load_shares(number_of, rows * top, most, skew, False)
    places = jnp.arange(number_of)

    def named(sizes, rotation):
        used = int((sizes > 0).sum())
        fixed = max(1, used // 4)
        passed = fixed + (places - fixed + rotation * (used - fixed)) % max(1, number_of - fixed)
        return jnp.zeros((number_of,), jnp.int32).at[order[jnp.where(places < fixed, places, passed)]].set(jnp.asarray(sizes, jnp.int32))

    sizes = jnp.where(number % 4 == 0, named(packed, number // 4), named(usual, number - number // 4 - 1))
    mixed = jax.random.permutation(jax.random.fold_in(own, 3), number_of)
    giver, receiver = mixed[0:number_of // 2 * 2:2], mixed[1:number_of // 2 * 2:2]
    room = jnp.minimum(sizes[giver] - 1, most - sizes[receiver]) // 2
    room = jnp.where((giver == order[0]) | (receiver == order[0]) | (sizes[receiver] == 0), 0, jnp.maximum(room, 0))
    passed = jax.random.randint(jax.random.fold_in(own, 4), (number_of // 2,), 0, 1 << 20) % (room + 1)
    sizes = sizes.at[giver].add(-passed).at[receiver].add(passed)
    labels = jnp.searchsorted(jnp.cumsum(sizes), jnp.arange(rows * top), side="right").astype(jnp.int32)
    table = labels.reshape(top, rows).T
    table = table[jax.random.permutation(jax.random.fold_in(own, 1), rows)]
    rotation = jax.random.randint(jax.random.fold_in(own, 2), (rows, 1), 0, top)
    return jnp.take_along_axis(table, (jnp.arange(top)[None, :] + rotation) % top, axis=1)


def load_shares(number_of, total, reach, slope, full):
    portions = [(1 << 20) // math.isqrt(grade ** slope) + 1 for grade in range(1, number_of + 1)]
    largest = reach if full else min(reach, max(-(-total // number_of), total * portions[0] // sum(portions)))
    least = 1 if total - largest >= number_of - 1 else 0
    counts, surplus = [largest] + [least] * (number_of - 1), total - largest - least * (number_of - 1)
    while surplus > 0:
        movable = [i for i in range(1, number_of) if counts[i] < largest] or [i for i in range(1, number_of) if counts[i] < reach]
        whole, left = sum([portions[i] for i in movable]), surplus
        for i in movable:
            extra = min(reach - counts[i], max(1, left * portions[i] // whole), surplus)
            counts[i] = counts[i] + extra
            surplus = surplus - extra
    return np.array(counts)


def normal_values(own_key, dims, width, limit, shards=(), kind=jnp.bfloat16):
    drawn = jax.random.normal(own_key, dims, jnp.float32) * width
    if len(shards) > 0:
        drawn = steps_of(own_key, dims, shards, -0.22, 0.18) * drawn
    return jnp.clip(drawn, min=-limit, max=limit).astype(kind)


def setup_inputs(seed: int = 0, part: int = 0) -> dict:
    keys = jax.random.split(jax.random.key(seed), 14)
    part_splits = jax.random.split(jax.random.fold_in(keys[13], part), 14)
    tokens = normal_values(part_splits[0], (TOKENS, D), 1.0, 6.0, ((0, 32),))
    queries = draw_queries(jax.random.fold_in(jax.random.fold_in(keys[13], part), 71), part)
    keys_local = normal_values(part_splits[2], (TOKENS, KVH * HD), 1.0, 6.0, ((0, 32),))
    values_local = normal_values(part_splits[3], (TOKENS, KVH * HD), 1.0, 6.0, ((0, 32),))
    prompt_keys = draw_prompt_keys(jax.random.fold_in(jax.random.fold_in(keys[13], part), 71), part)
    prompt_values = normal_values(part_splits[5], (PREFIX, KVH * HD), 1.0, 6.0)
    norm_gain = jnp.clip(1.0 + 0.15 * jax.random.normal(keys[6], (D,), jnp.float32), 0.25, 1.75)
    expert_ids_keys = jax.random.split(jax.random.fold_in(part_splits[7], 1), TOKENS // TOK_DEV)
    expert_ids_turns = jax.random.permutation(jax.random.fold_in(part_splits[7], 3), TOKENS // TOK_DEV)
    expert_ids = jax.vmap(lambda own, number: routed_block(jax.random.fold_in(part_splits[7], 2), own, number, TOK_DEV, EXPERTS, TOPK, CAP, 2))(expert_ids_keys, expert_ids_turns).reshape((TOKENS, TOPK))
    route_weight = jnp.clip(jnp.exp(math.log(1.0) - 2.9957323 * jax.random.uniform(part_splits[8], (TOKENS, TOPK), jnp.float32) ** steps_of(part_splits[8], (TOKENS, TOPK), ((0, 32),), -0.2, 0.2)), 0.05, 1.0)
    stored_gate = normal_values(keys[9], (EXPERTS, D, FFW), D ** -0.5, 0.09375, ((0, 16), (2, 2)))
    stored_up = normal_values(keys[10], (EXPERTS, D, FFW), D ** -0.5, 0.09375, ((0, 16), (2, 2)))
    stored_down = normal_values(keys[11], (EXPERTS, FFW, D), FFW ** -0.5, 0.21875, ((0, 16), (1, 2)))
    holder = draw_holder(jax.random.fold_in(keys[13], 71), part)
    return dict(tokens=tokens, queries=queries, keys_local=keys_local, values_local=values_local, prompt_keys=prompt_keys, prompt_values=prompt_values, norm_gain=norm_gain, expert_ids=expert_ids, route_weight=route_weight, stored_gate=stored_gate, stored_up=stored_up, stored_down=stored_down, holder=holder)


def attend_block(queries, keys_local, values_local, prompt_keys, prompt_values):
    count_rows = queries.shape[0]
    grouping = HEADS // KVH
    query_all = queries.astype(jnp.float32).reshape(count_rows, KVH, grouping, HD)
    key_all = jnp.concatenate([prompt_keys, keys_local], 0).astype(jnp.float32).reshape(-1, KVH, HD)
    value_all = jnp.concatenate([prompt_values, values_local], 0).astype(jnp.float32).reshape(-1, KVH, HD)
    scores = jnp.einsum('tkgd,skd->kgts', query_all, key_all) * HD ** (-0.5)
    column = jnp.arange(key_all.shape[0], dtype=jnp.int32)
    row_index = jnp.arange(count_rows, dtype=jnp.int32)
    allowed = (column[None, :] < PREFIX) | (column[None, :] - PREFIX <= row_index[:, None])
    scores = jnp.where(allowed[None, None], scores, -jnp.inf)
    highest = lax.optimization_barrier(jnp.max(scores, axis=-1, keepdims=True))
    expons = jnp.exp(scores - highest)
    weights = expons / lax.optimization_barrier(jnp.sum(expons, axis=-1, keepdims=True))
    weights = lax.optimization_barrier(weights.astype(jnp.bfloat16)).astype(jnp.float32)
    context = jnp.einsum('kgts,skd->tkgd', weights, value_all)
    return context.reshape(count_rows, HEADS * HD)

def reference(tokens, queries, keys_local, values_local, prompt_keys, prompt_values, norm_gain, expert_ids, route_weight, stored_gate, stored_up, stored_down, holder):
    block_count = TOKENS // TOK_DEV

    def one_block(items):
        return attend_block(items[0], items[1], items[2], prompt_keys, prompt_values)
    context = lax.map(one_block, (queries.reshape(block_count, TOK_DEV, -1), keys_local.reshape(block_count, TOK_DEV, -1), values_local.reshape(block_count, TOK_DEV, -1)))
    context = context.reshape(TOKENS, D)
    widened = tokens.astype(jnp.float32)
    normed = (widened * lax.rsqrt(lax.optimization_barrier(jnp.mean(widened * widened, axis=-1, keepdims=True)) + 1e-06) * norm_gain.astype(jnp.float32)).astype(jnp.bfloat16)
    shares = route_weight / lax.optimization_barrier(jnp.sum(route_weight, axis=-1, keepdims=True))
    grouped_ids = expert_ids.reshape(block_count, TOK_DEV * TOPK)
    onehot = (grouped_ids[:, :, None] == jnp.arange(EXPERTS, dtype=jnp.int32)[None, None, :]).astype(jnp.int32)
    slot_of = lax.optimization_barrier(jnp.sum((jnp.cumsum(onehot, axis=1) - onehot) * onehot, axis=2)).reshape(-1).astype(jnp.int32)
    flat_ids = expert_ids.reshape(-1).astype(jnp.int32)
    assigned = jnp.arange(TOKENS * TOPK, dtype=jnp.int32)
    anchor = (assigned // (TOK_DEV * TOPK)).astype(jnp.int32)
    token_of = (assigned // TOPK).astype(jnp.int32)
    column_at = anchor * CAP + slot_of
    row_table = jnp.full((EXPERTS, block_count * CAP), TOKENS, jnp.int32).at[flat_ids, column_at].set(token_of)
    share_table = jnp.zeros((EXPERTS, block_count * CAP), jnp.float32).at[flat_ids, column_at].set(shares.reshape(-1))
    padded = jnp.concatenate([normed, jnp.zeros((1, D), jnp.bfloat16)], 0)
    unit_count = FFW // SPLITS

    def serve(carry, inputs):
        expert_id, rows_at, scaling = inputs
        source = holder[expert_id]
        picked = padded[rows_at]
        gate_w = stored_gate[source]
        up_w = stored_up[source]
        down_w = stored_down[source]
        summed = jnp.zeros((picked.shape[0], D), jnp.float32)
        for section in range(SPLITS):
            lower = section * unit_count
            gate_val = jnp.dot(picked, gate_w[:, lower:lower + unit_count], preferred_element_type=jnp.float32)
            up_val = jnp.dot(picked, up_w[:, lower:lower + unit_count], preferred_element_type=jnp.float32)
            hidden = (jax.nn.silu(gate_val) * up_val).astype(jnp.bfloat16)
            partial_out = jnp.dot(hidden, down_w[lower:lower + unit_count], preferred_element_type=jnp.float32)
            summed = summed + lax.optimization_barrier(partial_out.astype(jnp.bfloat16)).astype(jnp.float32)
        result = lax.optimization_barrier(summed.astype(jnp.bfloat16)).astype(jnp.float32)
        carry = carry.at[rows_at].add(scaling[:, None] * result, mode='drop')
        return (carry, None)
    mixture, _ = lax.scan(serve, jnp.zeros((TOKENS, D), jnp.float32), (jnp.arange(EXPERTS, dtype=jnp.int32), row_table, share_table))
    return (widened + context + mixture).astype(jnp.bfloat16)
```

```python
import functools

import jax
import jax.numpy as jnp
from jax import lax
from jax.experimental import pallas as pl
from jax.experimental.pallas import tpu as pltpu
from jax.sharding import PartitionSpec as P

HEADS = 32
KVH = 2
HD = 128
PREFIX = 1024
LANES = 128


def attend_rows(queries, keys_local, values_local, prompt_keys, prompt_values):
    count_rows = queries.shape[0]
    grouping = HEADS // KVH
    query_all = queries.reshape(count_rows, KVH, grouping, HD)
    key_all = jnp.concatenate([prompt_keys, keys_local], 0).reshape(-1, KVH, HD)
    value_all = jnp.concatenate([prompt_values, values_local], 0).reshape(-1, KVH, HD)
    scores = jnp.einsum(
        "tkgd,skd->kgts", query_all, key_all, preferred_element_type=jnp.float32
    ) * HD ** (-0.5)
    column = jnp.arange(key_all.shape[0], dtype=jnp.int32)
    row_index = jnp.arange(count_rows, dtype=jnp.int32)
    prefix = prompt_keys.shape[0]
    allowed = (column[None, :] < prefix) | (column[None, :] - prefix <= row_index[:, None])
    scores = jnp.where(allowed[None, None], scores, -jnp.inf)
    highest = jnp.max(scores, axis=-1, keepdims=True)
    expons = jnp.exp(scores - highest)
    weights = (expons / jnp.sum(expons, axis=-1, keepdims=True)).astype(jnp.bfloat16)
    context = jnp.einsum("kgts,skd->tkgd", weights, value_all, preferred_element_type=jnp.float32)
    return context.reshape(count_rows, HEADS * HD)


def payload_kernel(experts, holder_ref, tokens_ref, gain_ref, ids_ref, route_ref, out_ref):
    width = tokens_ref.shape[1]
    wide = tokens_ref[...].astype(jnp.float32)
    scale = lax.rsqrt(jnp.mean(wide * wide, axis=-1, keepdims=True) + 1e-06)
    out_ref[:, :width] = (wide * scale * gain_ref[...]).astype(jnp.bfloat16)
    extra = out_ref.shape[1] - width
    rows = tokens_ref.shape[0]
    lane = lax.broadcasted_iota(jnp.int32, (rows, extra), 1)
    slot = lane % experts
    held = jnp.zeros((rows, extra), jnp.int32)
    for i in range(experts):
        held = jnp.where(slot == i, holder_ref[i], held)
    route = route_ref[...]
    share = route / jnp.sum(route, axis=-1, keepdims=True)
    per_slot = jnp.zeros((rows, extra), jnp.float32)
    for k in range(ids_ref.shape[1]):
        per_slot += jnp.where(ids_ref[:, k : k + 1] == held, share[:, k : k + 1], 0.0)
    high = per_slot.astype(jnp.bfloat16).astype(jnp.float32)
    both = jnp.where(lane < experts, high, jnp.where(lane < 2 * experts, per_slot - high, 0.0))
    out_ref[:, width:] = both.astype(jnp.bfloat16)


def make_payload(tokens, norm_gain, expert_ids, route_weight, holder):
    rows, width = tokens.shape
    experts = holder.shape[0]
    extra = -(-2 * experts // LANES) * LANES
    vmem = pl.BlockSpec(memory_space=pltpu.VMEM)
    return pl.pallas_call(
        functools.partial(payload_kernel, experts),
        out_shape=jax.ShapeDtypeStruct((rows, width + extra), jnp.bfloat16),
        in_specs=[pl.BlockSpec(memory_space=pltpu.SMEM)] + [vmem] * 4,
        out_specs=vmem,
        name="payload",
    )(holder, tokens, norm_gain.reshape(1, -1), expert_ids, route_weight)


STEPS = 4


def ffn_kernel(counts, experts, slot_ref, *refs):
    n = len(counts)
    blocks, refs = refs[:n], refs[n:]
    weights, refs = refs[:6], refs[6:]
    outs, refs = refs[:n], refs[n:]
    rows_buf, gu_buf, down_buf, hid_buf, row_sem, gu_sem, down_sem = refs
    gate_m, up_m, down_m, gate_p, up_p, down_p = weights
    width, half = gate_m.shape
    step = width // STEPS

    starts = [sum(counts[:i]) for i in range(n)]
    row_copies = [
        pltpu.make_async_copy(blocks[i], rows_buf.at[pl.ds(starts[i], counts[i])], row_sem.at[i])
        for i in range(n)
    ]
    gu_copies = []
    for side, (gate, up) in enumerate(((gate_m, up_m), (gate_p, up_p))):
        for s in range(STEPS):
            at = pl.ds(s * step, step)
            gu_copies.append(
                (
                    pltpu.make_async_copy(
                        gate.at[at], gu_buf.at[side, at, pl.ds(0, half)], gu_sem.at[side, s, 0]
                    ),
                    pltpu.make_async_copy(
                        up.at[at], gu_buf.at[side, at, pl.ds(half, half)], gu_sem.at[side, s, 1]
                    ),
                )
            )
    down_copies = [
        pltpu.make_async_copy(ref, down_buf.at[pl.ds(side * half, half)], down_sem.at[side])
        for side, ref in enumerate((down_m, down_p))
    ]
    for copy in row_copies:
        copy.start()
    for pair in gu_copies:
        for copy in pair:
            copy.start()
    for copy in down_copies:
        copy.start()
    for copy in row_copies:
        copy.wait()

    for side in range(2):
        total = None
        for s in range(STEPS):
            for copy in gu_copies[side * STEPS + s]:
                copy.wait()
            part = jnp.dot(
                rows_buf[:, s * step : (s + 1) * step],
                gu_buf[side, s * step : (s + 1) * step, :],
                preferred_element_type=jnp.float32,
            )
            total = part if total is None else total + part
        gate, up = total[:, :half], total[:, half:]
        hid_buf[:, side * half : (side + 1) * half] = (
            gate / (1.0 + jnp.exp(-gate)) * up
        ).astype(jnp.bfloat16)

    extra = rows_buf.shape[1] - width
    lane = lax.broadcasted_iota(jnp.int32, (rows_buf.shape[0], extra), 1)
    mine = (lane == slot_ref[0]) | (lane == slot_ref[0] + experts)
    share = jnp.sum(
        jnp.where(mine, rows_buf[:, width:].astype(jnp.float32), 0.0), axis=-1, keepdims=True
    )
    for copy in down_copies:
        copy.wait()
    for s in range(STEPS):
        at = slice(s * step, (s + 1) * step)
        result = jnp.dot(hid_buf[...], down_buf[:, at], preferred_element_type=jnp.float32)
        result = jnp.where(share == 0.0, 0.0, result * share).astype(jnp.bfloat16)
        for i in range(n):
            outs[i][:, at] = result[starts[i] : starts[i] + counts[i]]


def run_ffn(slot, blocks, weights, experts):
    counts = tuple(b.shape[0] for b in blocks)
    rows, padded = sum(counts), blocks[0].shape[1]
    width, half = weights[0].shape
    anyspace = pl.BlockSpec(memory_space=pl.ANY)
    return pl.pallas_call(
        functools.partial(ffn_kernel, counts, experts),
        out_shape=[jax.ShapeDtypeStruct((c, width), jnp.bfloat16) for c in counts],
        in_specs=[pl.BlockSpec(memory_space=pltpu.SMEM)] + [anyspace] * (len(blocks) + 6),
        out_specs=[pl.BlockSpec(memory_space=pltpu.VMEM)] * len(blocks),
        scratch_shapes=[
            pltpu.VMEM((rows, padded), jnp.bfloat16),
            pltpu.VMEM((2, width, 2 * half), jnp.bfloat16),
            pltpu.VMEM((2 * half, width), jnp.bfloat16),
            pltpu.VMEM((rows, 2 * half), jnp.bfloat16),
            pltpu.SemaphoreType.DMA((len(blocks),)),
            pltpu.SemaphoreType.DMA((2, STEPS, 2)),
            pltpu.SemaphoreType.DMA((2,)),
        ],
        compiler_params=pltpu.CompilerParams(vmem_limit_bytes=40 * 2**20),
        cost_estimate=pl.CostEstimate(
            flops=2 * rows * width * half * 6,
            bytes_accessed=12 * width * half + 4 * rows * width,
            transcendentals=rows * half * 2,
        ),
        name="ffn",
    )(slot, *blocks, *weights)


def local(
    tokens,
    queries,
    keys_local,
    values_local,
    prompt_keys,
    prompt_values,
    norm_gain,
    expert_ids,
    route_weight,
    stored_gate,
    stored_up,
    stored_down,
    holder,
):
    owners = lax.axis_size("expert")
    experts = holder.shape[0]
    columns = owners // 4
    f32, bf16 = jnp.float32, jnp.bfloat16

    def swap(value, offset):
        return lax.ppermute(value, "expert", [(i, i ^ offset) for i in range(owners)])

    def partner(value):
        return lax.ppermute(value, "dp", [(0, 1), (1, 0)])

    def add(*values):
        return sum(v.astype(f32) for v in values).astype(bf16)

    payload = make_payload(tokens, norm_gain, expert_ids, route_weight, holder)
    half = tokens.shape[0] // 2
    own_weights = (stored_gate[0], stored_up[0], stored_down[0])
    weights = own_weights + tuple(partner(w) for w in own_weights)
    slot = lax.axis_index("expert").astype(jnp.int32).reshape(1)

    sums = []
    for k in range(columns):
        base = payload if k == 0 else swap(payload, 4 * k)
        from_x, from_y = swap(base, 1), swap(base, 2)
        diag_top, diag_bot = swap(from_y[:half], 1), swap(from_x[half:], 2)
        own, for_x, for_y, top, bot = run_ffn(
            slot, (base, from_x, from_y, diag_top, diag_bot), weights, experts
        )
        top, bot = swap(top, 1), swap(bot, 2)
        for_y = jnp.concatenate([add(for_y[:half], top), for_y[half:]], 0)
        for_x = jnp.concatenate([for_x[:half], add(for_x[half:], bot)], 0)
        total = add(own, swap(for_x, 1), swap(for_y, 2))
        sums.append(total if k == 0 else swap(total, 4 * k))
    context = attend_rows(queries, keys_local, values_local, prompt_keys, prompt_values)
    result = tokens.astype(f32) + context
    for part in sums:
        result = result + part.astype(f32)
    return result.astype(bf16)


def solution(mesh):
    return jax.shard_map(
        local,
        mesh=mesh,
        in_specs=(
            P(("group", "expert", "dp"), None),
            P(("group", "expert", "dp"), None),
            P(("group", "expert", "dp"), None),
            P(("group", "expert", "dp"), None),
            P("group", None),
            P("group", None),
            P(),
            P(("group", "expert", "dp"), None),
            P(("group", "expert", "dp"), None),
            P("expert", None, "dp"),
            P("expert", None, "dp"),
            P("expert", "dp", None),
            P(),
        ),
        out_specs=P(("group", "expert", "dp"), None),
        check_vma=False,
    )
```

```python
import functools

import jax
import jax.numpy as jnp
from jax import lax
from jax.experimental import pallas as pl
from jax.experimental.pallas import tpu as pltpu
from jax.sharding import PartitionSpec as P

HEADS = 32
KVH = 2
HD = 128
PREFIX = 1024
LANES = 128


def attend_kernel(heads, q_ref, keys_ref, values_ref, pkeys_ref, pvalues_ref, tokens_ref, out_ref):
    rows = q_ref.shape[0]
    prefix = pkeys_ref.shape[0]
    dims = (((1,), (1,)), ((), ()))
    scale = HD ** (-0.5)
    stacked = jnp.concatenate([q_ref[:, h * HD : (h + 1) * HD] for h in range(heads)], 0)
    first = lax.dot_general(stacked, pkeys_ref[...], dims, preferred_element_type=jnp.float32)
    last = lax.dot_general(stacked, keys_ref[...], dims, preferred_element_type=jnp.float32)
    query = lax.broadcasted_iota(jnp.int32, (rows, rows), 0)
    key = lax.broadcasted_iota(jnp.int32, (rows, rows), 1)
    allowed = jnp.concatenate([key <= query] * heads, 0)
    first = first * scale
    last = jnp.where(allowed, last * scale, -jnp.inf)
    highest = jnp.maximum(
        jnp.max(first, axis=-1, keepdims=True), jnp.max(last, axis=-1, keepdims=True)
    )
    first, last = jnp.exp(first - highest), jnp.exp(last - highest)
    total = jnp.sum(first, axis=-1, keepdims=True) + jnp.sum(last, axis=-1, keepdims=True)
    inverse = 1.0 / total
    context = jnp.dot(
        (first * inverse).astype(jnp.bfloat16), pvalues_ref[...], preferred_element_type=jnp.float32
    ) + jnp.dot(
        (last * inverse).astype(jnp.bfloat16), values_ref[...], preferred_element_type=jnp.float32
    )
    for h in range(heads):
        at = slice(h * HD, (h + 1) * HD)
        out_ref[:, at] = tokens_ref[:, at].astype(jnp.float32) + context[h * rows : (h + 1) * rows]


def attend(tokens, queries, keys_local, values_local, prompt_keys, prompt_values, heads=4):
    rows, width = tokens.shape
    prefix = prompt_keys.shape[0]
    per_key = HEADS // KVH // heads
    wide = pl.BlockSpec((rows, heads * HD), lambda i: (0, i))
    own = pl.BlockSpec((rows, HD), lambda i: (0, i // per_key))
    shared = pl.BlockSpec((prefix, HD), lambda i: (0, i // per_key))
    return pl.pallas_call(
        functools.partial(attend_kernel, heads),
        grid=(HEADS // heads,),
        out_shape=jax.ShapeDtypeStruct((rows, width), jnp.float32),
        in_specs=[wide, own, own, shared, shared, wide],
        out_specs=wide,
        compiler_params=pltpu.CompilerParams(vmem_limit_bytes=24 * 2**20),
        cost_estimate=pl.CostEstimate(
            flops=4 * rows * (prefix + rows) * width,
            bytes_accessed=8 * rows * width,
            transcendentals=rows * (prefix + rows) * HEADS,
        ),
        name="attend",
    )(queries, keys_local, values_local, prompt_keys, prompt_values, tokens)


def payload_kernel(experts, holder_ref, tokens_ref, gain_ref, ids_ref, route_ref, out_ref):
    rows, width = tokens_ref.shape
    wide = tokens_ref[...].astype(jnp.float32)
    scale = lax.rsqrt(jnp.mean(wide * wide, axis=-1, keepdims=True) + 1e-06)
    out_ref[:, :width] = (wide * scale * gain_ref[...]).astype(jnp.bfloat16)
    extra = out_ref.shape[1] - width
    part = lax.broadcasted_iota(jnp.int32, (extra, rows), 0)
    slot = part % experts
    held = jnp.zeros((extra, rows), jnp.int32)
    for i in range(experts):
        held = jnp.where(slot == i, holder_ref[i], held)
    route = route_ref[...]
    share = route / jnp.sum(route, axis=0, keepdims=True)
    per_slot = jnp.zeros((extra, rows), jnp.float32)
    for k in range(ids_ref.shape[0]):
        per_slot += jnp.where(ids_ref[k : k + 1] == held, share[k : k + 1], 0.0)
    high = per_slot.astype(jnp.bfloat16).astype(jnp.float32)
    both = jnp.where(part < experts, high, jnp.where(part < 2 * experts, per_slot - high, 0.0))
    same = lax.broadcasted_iota(jnp.int32, (rows, rows), 0) == lax.broadcasted_iota(
        jnp.int32, (rows, rows), 1
    )
    turned = lax.dot_general(
        same.astype(jnp.bfloat16),
        both.astype(jnp.bfloat16),
        (((1,), (1,)), ((), ())),
        preferred_element_type=jnp.float32,
    )
    out_ref[:, width:] = turned.astype(jnp.bfloat16)


def make_payload(tokens, norm_gain, expert_ids, route_weight, holder):
    rows, width = tokens.shape
    experts = holder.shape[0]
    extra = -(-2 * experts // LANES) * LANES
    vmem = pl.BlockSpec(memory_space=pltpu.VMEM)
    return pl.pallas_call(
        functools.partial(payload_kernel, experts),
        out_shape=jax.ShapeDtypeStruct((rows, width + extra), jnp.bfloat16),
        in_specs=[pl.BlockSpec(memory_space=pltpu.SMEM)] + [vmem] * 4,
        out_specs=vmem,
        name="payload",
    )(holder, tokens, norm_gain.reshape(1, -1), expert_ids.T, route_weight.T)


STEPS = 4


def ffn_kernel(counts, experts, slot_ref, *refs):
    n = len(counts)
    blocks, refs = refs[:n], refs[n:]
    weights, refs = refs[:6], refs[6:]
    outs, refs = refs[:n], refs[n:]
    rows_buf, gu_buf, down_buf, acc_buf, hid_buf, row_sem, gu_sem, down_sem = refs
    gate_m, up_m, down_m, gate_p, up_p, down_p = weights
    width, half = gate_m.shape
    step = width // STEPS
    starts = [sum(counts[:i]) for i in range(n)]

    row_copies = [
        pltpu.make_async_copy(blocks[i], rows_buf.at[pl.ds(starts[i], counts[i])], row_sem.at[i])
        for i in range(n)
    ]

    def gu_copies(side, s):
        at = pl.ds(pl.multiple_of(s * step, step), step)
        pair = ((gate_m, up_m), (gate_p, up_p))[side]
        return [
            pltpu.make_async_copy(
                ref.at[at], gu_buf.at[side, at, pl.ds(j * half, half)], gu_sem.at[side, s, j]
            )
            for j, ref in enumerate(pair)
        ]

    down_copies = [
        pltpu.make_async_copy(ref, down_buf.at[pl.ds(side * half, half)], down_sem.at[side])
        for side, ref in enumerate((down_m, down_p))
    ]
    for copy in row_copies:
        copy.start()
    for side in range(2):
        for s in range(STEPS):
            for copy in gu_copies(side, s):
                copy.start()
    for copy in down_copies:
        copy.start()
    for copy in row_copies:
        copy.wait()

    for side in range(2):

        def grow(s, carry, side=side):
            for copy in gu_copies(side, s):
                copy.wait()
            at = pl.ds(pl.multiple_of(s * step, step), step)
            part = jnp.dot(
                rows_buf[:, at], gu_buf[side, at, :], preferred_element_type=jnp.float32
            )

            @pl.when(s == 0)
            def _():
                acc_buf[...] = part

            @pl.when(s > 0)
            def _():
                acc_buf[...] += part

            return carry

        lax.fori_loop(0, STEPS, grow, 0)
        gate, up = acc_buf[:, :half], acc_buf[:, half:]
        hid_buf[:, side * half : (side + 1) * half] = (
            gate / (1.0 + jnp.exp(-gate)) * up
        ).astype(jnp.bfloat16)

    extra = rows_buf.shape[1] - width
    lane = lax.broadcasted_iota(jnp.int32, (rows_buf.shape[0], extra), 1)
    mine = (lane == slot_ref[0]) | (lane == slot_ref[0] + experts)
    share = jnp.sum(
        jnp.where(mine, rows_buf[:, width:].astype(jnp.float32), 0.0), axis=-1, keepdims=True
    )
    for copy in down_copies:
        copy.wait()

    def finish(s, carry):
        at = pl.ds(pl.multiple_of(s * step, step), step)
        result = jnp.dot(hid_buf[...], down_buf[:, at], preferred_element_type=jnp.float32)
        result = jnp.where(share == 0.0, 0.0, result * share).astype(jnp.bfloat16)
        for i in range(n):
            outs[i][:, at] = result[starts[i] : starts[i] + counts[i]]
        return carry

    lax.fori_loop(0, STEPS, finish, 0)


def run_ffn(slot, blocks, weights, experts):
    counts = tuple(b.shape[0] for b in blocks)
    rows, padded = sum(counts), blocks[0].shape[1]
    width, half = weights[0].shape
    anyspace = pl.BlockSpec(memory_space=pl.ANY)
    return pl.pallas_call(
        functools.partial(ffn_kernel, counts, experts),
        out_shape=[jax.ShapeDtypeStruct((c, width), jnp.bfloat16) for c in counts],
        in_specs=[pl.BlockSpec(memory_space=pltpu.SMEM)] + [anyspace] * (len(blocks) + 6),
        out_specs=[pl.BlockSpec(memory_space=pltpu.VMEM)] * len(blocks),
        scratch_shapes=[
            pltpu.VMEM((rows, padded), jnp.bfloat16),
            pltpu.VMEM((2, width, 2 * half), jnp.bfloat16),
            pltpu.VMEM((2 * half, width), jnp.bfloat16),
            pltpu.VMEM((rows, 2 * half), jnp.float32),
            pltpu.VMEM((rows, 2 * half), jnp.bfloat16),
            pltpu.SemaphoreType.DMA((len(blocks),)),
            pltpu.SemaphoreType.DMA((2, STEPS, 2)),
            pltpu.SemaphoreType.DMA((2,)),
        ],
        compiler_params=pltpu.CompilerParams(vmem_limit_bytes=56 * 2**20),
        cost_estimate=pl.CostEstimate(
            flops=2 * rows * width * half * 6,
            bytes_accessed=12 * width * half + 4 * rows * width,
            transcendentals=rows * half * 2,
        ),
        name="ffn",
    )(slot, *blocks, *weights)


def after(value, *others):
    return lax.optimization_barrier((value,) + others)[0]


def local(
    tokens,
    queries,
    keys_local,
    values_local,
    prompt_keys,
    prompt_values,
    norm_gain,
    expert_ids,
    route_weight,
    stored_gate,
    stored_up,
    stored_down,
    holder,
):
    owners = lax.axis_size("expert")
    experts = holder.shape[0]
    columns = owners // 4
    f32, bf16 = jnp.float32, jnp.bfloat16

    def swap(value, offset):
        return lax.ppermute(value, "expert", [(i, i ^ offset) for i in range(owners)])

    def partner(value):
        return lax.ppermute(value, "dp", [(0, 1), (1, 0)])

    def add(*values):
        return sum(v.astype(f32) for v in values).astype(bf16)

    payload = make_payload(tokens, norm_gain, expert_ids, route_weight, holder)
    own_weights = (stored_gate[0], stored_up[0], stored_down[0])
    weights = own_weights + tuple(partner(w) for w in own_weights)
    slot = lax.axis_index("expert").astype(jnp.int32).reshape(1)

    def spread(base, k):
        from_x, from_y = swap(base, 1), swap(base, 2)
        diagonal = swap(from_y, 1) if k % 2 == 0 else swap(from_x, 2)
        return [base, from_x, from_y, diagonal]

    def collect(parts, k):
        own, for_x, for_y, diagonal = parts
        if k % 2 == 0:
            for_y = add(for_y, swap(diagonal, 1))
        else:
            for_x = add(for_x, swap(diagonal, 2))
        parts = [own, swap(for_x, 1), swap(for_y, 2)]
        return parts if k == 0 else [swap(add(*parts), 4 * k)]

    blocks, last = [], payload
    for k in range(columns):
        if k == 0:
            base = payload
        else:
            base = swap(after(payload, last) if k > 2 else payload, 4 * k)
            if k != 1:
                last = base
        blocks.append(spread(base, k))
    outs = []
    for k in range(0, columns, 2):
        both = run_ffn(slot, blocks[k] + blocks[k + 1], weights, experts)
        outs += [both[:4], both[4:]]
    parts = []
    for k in list(range(1, columns)) + [0]:
        parts += collect(outs[k], k)
    result = attend(tokens, queries, keys_local, values_local, prompt_keys, prompt_values)
    for part in parts:
        result = result + part.astype(f32)
    return result.astype(bf16)


def solution(mesh):
    return jax.shard_map(
        local,
        mesh=mesh,
        in_specs=(
            P(("group", "expert", "dp"), None),
            P(("group", "expert", "dp"), None),
            P(("group", "expert", "dp"), None),
            P(("group", "expert", "dp"), None),
            P("group", None),
            P("group", None),
            P(),
            P(("group", "expert", "dp"), None),
            P(("group", "expert", "dp"), None),
            P("expert", None, "dp"),
            P("expert", None, "dp"),
            P("expert", "dp", None),
            P(),
        ),
        out_specs=P(("group", "expert", "dp"), None),
        check_vma=False,
    )
```

```python
import functools

import jax
import jax.numpy as jnp
from jax import lax
from jax.experimental import pallas as pl
from jax.experimental.pallas import tpu as pltpu
from jax.sharding import PartitionSpec as P


HEADS = 32
KVH = 2
HD = 128
TOPK = 8
LANES = 128


def attend_kernel(heads, q_ref, keys_ref, values_ref, pkeys_ref, pvalues_ref, tokens_ref, out_ref):
    rows = q_ref.shape[0]
    dims = (((1,), (1,)), ((), ()))
    scale = HD ** (-0.5)
    stacked = jnp.concatenate([q_ref[:, h * HD : (h + 1) * HD] for h in range(heads)], 0)
    first = lax.dot_general(stacked, pkeys_ref[...], dims, preferred_element_type=jnp.float32)
    last = lax.dot_general(stacked, keys_ref[...], dims, preferred_element_type=jnp.float32)
    query = lax.broadcasted_iota(jnp.int32, (rows, rows), 0)
    key = lax.broadcasted_iota(jnp.int32, (rows, rows), 1)
    allowed = jnp.concatenate([key <= query] * heads, 0)
    first = first * scale
    last = jnp.where(allowed, last * scale, -jnp.inf)
    highest = jnp.maximum(
        jnp.max(first, axis=-1, keepdims=True), jnp.max(last, axis=-1, keepdims=True)
    )
    first, last = jnp.exp(first - highest), jnp.exp(last - highest)
    total = jnp.sum(first, axis=-1, keepdims=True) + jnp.sum(last, axis=-1, keepdims=True)
    inverse = 1.0 / total
    context = jnp.dot(
        (first * inverse).astype(jnp.bfloat16), pvalues_ref[...], preferred_element_type=jnp.float32
    ) + jnp.dot(
        (last * inverse).astype(jnp.bfloat16), values_ref[...], preferred_element_type=jnp.float32
    )
    for h in range(heads):
        at = slice(h * HD, (h + 1) * HD)
        out_ref[:, at] = tokens_ref[:, at].astype(jnp.float32) + context[h * rows : (h + 1) * rows]


def attend(tokens, queries, keys_local, values_local, prompt_keys, prompt_values, heads=4):
    rows, width = tokens.shape
    prefix = prompt_keys.shape[0]
    per_key = HEADS // KVH // heads
    wide = pl.BlockSpec((rows, heads * HD), lambda i: (0, i))
    own = pl.BlockSpec((rows, HD), lambda i: (0, i // per_key))
    shared = pl.BlockSpec((prefix, HD), lambda i: (0, i // per_key))
    return pl.pallas_call(
        functools.partial(attend_kernel, heads),
        grid=(HEADS // heads,),
        out_shape=jax.ShapeDtypeStruct((rows, width), jnp.float32),
        in_specs=[wide, own, own, shared, shared, wide],
        out_specs=wide,
        compiler_params=pltpu.CompilerParams(vmem_limit_bytes=VMEM_LIMIT),
        cost_estimate=pl.CostEstimate(
            flops=4 * rows * (prefix + rows) * width,
            bytes_accessed=8 * rows * width,
            transcendentals=rows * (prefix + rows) * HEADS,
        ),
        name="attend",
    )(queries, keys_local, values_local, prompt_keys, prompt_values, tokens)


def payload_kernel(experts, holder_ref, tokens_ref, gain_ref, ids_ref, route_ref, out_ref):
    rows, width = tokens_ref.shape
    wide = tokens_ref[...].astype(jnp.float32)
    scale = lax.rsqrt(jnp.mean(wide * wide, axis=-1, keepdims=True) + 1e-06)
    out_ref[:, :width] = (wide * scale * gain_ref[...]).astype(jnp.bfloat16)
    extra = out_ref.shape[1] - width
    part = lax.broadcasted_iota(jnp.int32, (extra, rows), 0)
    slot = part % experts
    held = jnp.zeros((extra, rows), jnp.int32)
    for i in range(experts):
        held = jnp.where(slot == i, holder_ref[i], held)
    route = route_ref[...]
    share = route / jnp.sum(route, axis=0, keepdims=True)
    per_slot = jnp.zeros((extra, rows), jnp.float32)
    for k in range(ids_ref.shape[0]):
        per_slot += jnp.where(ids_ref[k : k + 1] == held, share[k : k + 1], 0.0)
    high = per_slot.astype(jnp.bfloat16).astype(jnp.float32)
    both = jnp.where(part < experts, high, jnp.where(part < 2 * experts, per_slot - high, 0.0))
    same = lax.broadcasted_iota(jnp.int32, (rows, rows), 0) == lax.broadcasted_iota(
        jnp.int32, (rows, rows), 1
    )
    turned = lax.dot_general(
        same.astype(jnp.bfloat16),
        both.astype(jnp.bfloat16),
        (((1,), (1,)), ((), ())),
        preferred_element_type=jnp.float32,
    )
    out_ref[:, width:] = turned.astype(jnp.bfloat16)


def make_payload(tokens, norm_gain, expert_ids, route_weight, holder):
    rows, width = tokens.shape
    experts = holder.shape[0]
    extra = -(-2 * experts // LANES) * LANES
    vmem = pl.BlockSpec(memory_space=pltpu.VMEM)
    return pl.pallas_call(
        functools.partial(payload_kernel, experts),
        out_shape=jax.ShapeDtypeStruct((rows, width + extra), jnp.bfloat16),
        in_specs=[pl.BlockSpec(memory_space=pltpu.SMEM)] + [vmem] * 4,
        out_specs=vmem,
        name="payload",
    )(holder, tokens, norm_gain.reshape(1, -1), expert_ids.T, route_weight.T)


PLANE = 4
CHUNK = 1024
SLICE = 128
VMEM_LIMIT = 60 * 2**20


def capacity(tokens, owners):
    return min(tokens, max(2, tokens * TOPK * 4 // (3 * owners)))


def chunks(width):
    return [slice(at, min(at + CHUNK, width)) for at in range(0, width, CHUNK)]


def dispatch_kernel(slot_ref, base_ref, *outs):
    tokens, padded = base_ref.shape
    count = outs[0].shape[0]
    width = padded - padded % CHUNK
    extra = padded - width
    row = lax.broadcasted_iota(jnp.int32, (tokens, tokens), 0)
    column = lax.broadcasted_iota(jnp.int32, (tokens, tokens), 1)
    turned = lax.dot_general(
        base_ref[:, width:],
        (row == column).astype(jnp.bfloat16),
        (((0,), (0,)), ((), ())),
        preferred_element_type=jnp.float32,
    )
    part = lax.broadcasted_iota(jnp.int32, (extra, tokens), 0)
    routed = [
        jnp.sum(jnp.where(part == (slot_ref[0] ^ j), turned, 0.0), axis=0, keepdims=True) > 0.0
        for j in range(PLANE)
    ]
    ones = jnp.concatenate([r.astype(jnp.float32) for r in routed] * 2, 0).astype(jnp.bfloat16)
    place = jnp.dot(ones, (row < column).astype(jnp.bfloat16), preferred_element_type=jnp.float32)
    target = lax.broadcasted_iota(jnp.int32, (count, tokens), 0)
    chooser = jnp.concatenate(
        [
            jnp.where(
                (target == place[j : j + 1].astype(jnp.int32)) & routed[j], 1.0, 0.0
            ).astype(jnp.bfloat16)
            for j in range(PLANE)
        ],
        0,
    )
    for at in chunks(padded):
        rows = jnp.dot(chooser, base_ref[:, at], preferred_element_type=jnp.float32)
        rows = rows.astype(jnp.bfloat16)
        for j in range(PLANE):
            outs[j][:, at] = rows[j * count : (j + 1) * count]


def dispatch(slot, base, count):
    vmem = pl.BlockSpec(memory_space=pltpu.VMEM)
    tokens, padded = base.shape
    return pl.pallas_call(
        dispatch_kernel,
        out_shape=[jax.ShapeDtypeStruct((count, padded), jnp.bfloat16)] * PLANE,
        in_specs=[pl.BlockSpec(memory_space=pltpu.SMEM), vmem],
        out_specs=[vmem] * PLANE,
        cost_estimate=pl.CostEstimate(
            flops=2 * PLANE * count * tokens * padded,
            bytes_accessed=2 * (tokens + PLANE * count) * padded,
            transcendentals=0,
        ),
        name="dispatch",
    )(slot, base)


def combine_kernel(extras, slot_ref, meta_ref, *refs):
    results, terms, out_ref = refs[:PLANE], refs[PLANE : PLANE + extras], refs[-1]
    tokens, extra = meta_ref.shape
    count, width = results[0].shape
    row = lax.broadcasted_iota(jnp.int32, (tokens, tokens), 0)
    column = lax.broadcasted_iota(jnp.int32, (tokens, tokens), 1)
    lane = lax.broadcasted_iota(jnp.int32, (tokens, extra), 1)
    meta = meta_ref[...].astype(jnp.float32)
    before = (column < row).astype(jnp.bfloat16)
    target = lax.broadcasted_iota(jnp.int32, (tokens, count), 1)
    chooser = []
    for j in range(PLANE):
        routed = (
            jnp.sum(jnp.where(lane == (slot_ref[0] ^ j), meta, 0.0), axis=1, keepdims=True) > 0.0
        )
        ones = jnp.broadcast_to(jnp.where(routed, 1.0, 0.0), (tokens, count)).astype(jnp.bfloat16)
        place = jnp.dot(before, ones, preferred_element_type=jnp.float32)
        chooser.append(
            jnp.where((target == place.astype(jnp.int32)) & routed, 1.0, 0.0).astype(jnp.bfloat16)
        )
    chooser = jnp.concatenate(chooser, 1)
    for at in chunks(width):
        rows = jnp.concatenate([r[:, at] for r in results], 0)
        total = jnp.dot(chooser, rows, preferred_element_type=jnp.float32)
        for term in terms:
            total = total + term[:, at].astype(jnp.float32)
        out_ref[:, at] = total.astype(out_ref.dtype)


def combine(slot, base, results, terms, dtype):
    tokens, padded = base.shape
    count, width = results[0].shape
    extra = padded - width
    whole = lambda a: pl.BlockSpec(a.shape, lambda i: (0, 0))
    return pl.pallas_call(
        functools.partial(combine_kernel, len(terms)),
        grid=(1,),
        out_shape=jax.ShapeDtypeStruct((tokens, width), dtype),
        in_specs=[
            pl.BlockSpec(memory_space=pltpu.SMEM),
            pl.BlockSpec((tokens, extra), lambda i: (0, width // extra)),
        ]
        + [whole(a) for a in (*results, *terms)],
        out_specs=pl.BlockSpec((tokens, width), lambda i: (0, 0)),
        cost_estimate=pl.CostEstimate(
            flops=2 * PLANE * count * tokens * width,
            bytes_accessed=2 * (tokens + PLANE * count) * width,
            transcendentals=0,
        ),
        name="combine",
    )(slot, base, *results, *terms)


def ffn_kernel(counts, experts, slot_ref, *refs):
    n = len(counts)
    blocks, refs = refs[:n], refs[n:]
    weights, refs = refs[:6], refs[6:]
    outs, refs = refs[:n], refs[n:]
    rows_buf, gu_buf, down_buf, hid_buf, row_sem, gu_sem, down_sem = refs
    gate_m, up_m, down_m, gate_p, up_p, down_p = weights
    width, half = gate_m.shape
    parts = half // SLICE
    starts = [sum(counts[:i]) for i in range(n)]

    row_copies = [
        pltpu.make_async_copy(blocks[i], rows_buf.at[pl.ds(starts[i], counts[i])], row_sem.at[i])
        for i in range(n)
    ]
    gu_copies = []
    for side, pair in enumerate(((gate_m, up_m), (gate_p, up_p))):
        for s in range(parts):
            gu_copies.append(
                [
                    pltpu.make_async_copy(
                        ref.at[:, pl.ds(s * SLICE, SLICE)],
                        gu_buf.at[side * parts + s, :, pl.ds(j * SLICE, SLICE)],
                        gu_sem.at[side * parts + s, j],
                    )
                    for j, ref in enumerate(pair)
                ]
            )
    down_copies = [
        pltpu.make_async_copy(ref, down_buf.at[pl.ds(side * half, half)], down_sem.at[side])
        for side, ref in enumerate((down_m, down_p))
    ]
    for copy in row_copies:
        copy.start()
    for pair in gu_copies:
        for copy in pair:
            copy.start()
    for copy in down_copies:
        copy.start()
    for copy in row_copies:
        copy.wait()

    for s, pair in enumerate(gu_copies):
        for copy in pair:
            copy.wait()
        both = jnp.dot(rows_buf[:, :width], gu_buf[s], preferred_element_type=jnp.float32)
        gate, up = both[:, :SLICE], both[:, SLICE:]
        hid_buf[:, s * SLICE : (s + 1) * SLICE] = (
            gate / (1.0 + jnp.exp(-gate)) * up
        ).astype(jnp.bfloat16)

    extra = rows_buf.shape[1] - width
    lane = lax.broadcasted_iota(jnp.int32, (rows_buf.shape[0], extra), 1)
    mine = (lane == slot_ref[0]) | (lane == slot_ref[0] + experts)
    share = jnp.sum(
        jnp.where(mine, rows_buf[:, width:].astype(jnp.float32), 0.0), axis=-1, keepdims=True
    )
    for copy in down_copies:
        copy.wait()
    for at in chunks(width):
        result = jnp.dot(hid_buf[...], down_buf[:, at], preferred_element_type=jnp.float32)
        result = (result * share).astype(jnp.bfloat16)
        for i in range(n):
            outs[i][:, at] = result[starts[i] : starts[i] + counts[i]]


def run_ffn(slot, blocks, weights, experts):
    counts = tuple(b.shape[0] for b in blocks)
    rows, padded = sum(counts), blocks[0].shape[1]
    width, half = weights[0].shape
    anyspace = pl.BlockSpec(memory_space=pl.ANY)
    parts = 2 * half // SLICE
    return pl.pallas_call(
        functools.partial(ffn_kernel, counts, experts),
        out_shape=[jax.ShapeDtypeStruct((c, width), jnp.bfloat16) for c in counts],
        in_specs=[pl.BlockSpec(memory_space=pltpu.SMEM)] + [anyspace] * (len(blocks) + 6),
        out_specs=[pl.BlockSpec(memory_space=pltpu.VMEM)] * len(blocks),
        scratch_shapes=[
            pltpu.VMEM((rows, padded), jnp.bfloat16),
            pltpu.VMEM((parts, width, 2 * SLICE), jnp.bfloat16),
            pltpu.VMEM((2 * half, width), jnp.bfloat16),
            pltpu.VMEM((rows, 2 * half), jnp.bfloat16),
            pltpu.SemaphoreType.DMA((len(blocks),)),
            pltpu.SemaphoreType.DMA((parts, 2)),
            pltpu.SemaphoreType.DMA((2,)),
        ],
        compiler_params=pltpu.CompilerParams(vmem_limit_bytes=VMEM_LIMIT),
        cost_estimate=pl.CostEstimate(
            flops=2 * rows * width * half * 6,
            bytes_accessed=12 * width * half + 4 * rows * width,
            transcendentals=rows * half * 2,
        ),
        name="ffn",
    )(slot, *blocks, *weights)


def after(value, *others):
    return lax.optimization_barrier((value,) + others)[0]


def local(
    tokens,
    queries,
    keys_local,
    values_local,
    prompt_keys,
    prompt_values,
    norm_gain,
    expert_ids,
    route_weight,
    stored_gate,
    stored_up,
    stored_down,
    holder,
):
    owners = lax.axis_size("expert")
    experts = holder.shape[0]
    columns = owners // 4
    f32, bf16 = jnp.float32, jnp.bfloat16

    def swap(value, offset):
        return lax.ppermute(value, "expert", [(i, i ^ offset) for i in range(owners)])

    def partner(value):
        return lax.ppermute(value, "dp", [(0, 1), (1, 0)])

    own_weights = (stored_gate[0], stored_up[0], stored_down[0])
    weights = own_weights + tuple(partner(w) for w in own_weights)
    payload = make_payload(tokens, norm_gain, expert_ids, route_weight, holder)
    slot = lax.axis_index("expert").astype(jnp.int32).reshape(1)

    rows = -(-capacity(tokens.shape[0], owners) // 16) * 16
    bases, blocks, outs = {}, {}, {}

    def gather(k, base):
        bases[k] = base
        own, to_x, to_y, to_d = dispatch(slot, base, rows)
        blocks[k] = (own, swap(to_x, 1), swap(to_y, 2), swap(to_d, 3))

    def serve(k):
        own, to_x, to_y, to_d = run_ffn(slot, blocks[k], weights, experts)
        outs[k] = (own, swap(to_x, 1), swap(to_y, 2), swap(to_d, 3))

    def collect(k, terms=(), dtype=bf16):
        return combine(slot, bases[k], outs[k], terms, dtype)

    gather(0, payload)
    result = attend(tokens, queries, keys_local, values_local, prompt_keys, prompt_values)
    for first in range(0, columns, 4):
        if first == 0:
            gather(1, swap(payload, 4))
            gather(2, swap(after(payload, bases[1]), 8))
        else:
            gather(first, swap(payload, 4 * first))
            gather(first + 1, swap(payload, 4 * first + 4))
            gather(first + 2, swap(payload, 4 * first + 8))
        gather(first + 3, swap(bases[first + 2], 4))
    for k in range(columns):
        serve(k)
    sums = []
    for first in range(0, columns, 4):
        sums.append(swap(collect(first + 1), 4 * first + 4))
        passed = swap(collect(first + 3), 4)
        sums.append(swap(collect(first + 2, (passed,)), 4 * first + 8))
        if first:
            sums.append(swap(collect(first), 4 * first))
    result = collect(0, (result,), f32)
    for part in sums:
        result = result + part.astype(f32)
    return result.astype(bf16)


def solution(mesh):
    return jax.shard_map(
        local,
        mesh=mesh,
        in_specs=(
            P(("group", "expert", "dp"), None),
            P(("group", "expert", "dp"), None),
            P(("group", "expert", "dp"), None),
            P(("group", "expert", "dp"), None),
            P("group", None),
            P("group", None),
            P(),
            P(("group", "expert", "dp"), None),
            P(("group", "expert", "dp"), None),
            P("expert", None, "dp"),
            P("expert", None, "dp"),
            P("expert", "dp", None),
            P(),
        ),
        out_specs=P(("group", "expert", "dp"), None),
        check_vma=False,
    )
```

```python
import functools

import jax
import jax.numpy as jnp
from jax import lax
from jax.experimental import pallas as pl
from jax.experimental.pallas import tpu as pltpu
from jax.sharding import PartitionSpec as P


HEADS = 32
KVH = 2
HD = 128
TOPK = 8
LANES = 128


def attend_kernel(heads, q_ref, keys_ref, values_ref, pkeys_ref, pvalues_ref, tokens_ref, out_ref):
    rows = q_ref.shape[0]
    dims = (((1,), (1,)), ((), ()))
    scale = HD ** (-0.5)
    stacked = jnp.concatenate([q_ref[:, h * HD : (h + 1) * HD] for h in range(heads)], 0)
    first = lax.dot_general(stacked, pkeys_ref[...], dims, preferred_element_type=jnp.float32)
    last = lax.dot_general(stacked, keys_ref[...], dims, preferred_element_type=jnp.float32)
    query = lax.broadcasted_iota(jnp.int32, (rows, rows), 0)
    key = lax.broadcasted_iota(jnp.int32, (rows, rows), 1)
    allowed = jnp.concatenate([key <= query] * heads, 0)
    first = first * scale
    last = jnp.where(allowed, last * scale, -jnp.inf)
    highest = jnp.maximum(
        jnp.max(first, axis=-1, keepdims=True), jnp.max(last, axis=-1, keepdims=True)
    )
    first, last = jnp.exp(first - highest), jnp.exp(last - highest)
    total = jnp.sum(first, axis=-1, keepdims=True) + jnp.sum(last, axis=-1, keepdims=True)
    inverse = 1.0 / total
    context = jnp.dot(
        (first * inverse).astype(jnp.bfloat16), pvalues_ref[...], preferred_element_type=jnp.float32
    ) + jnp.dot(
        (last * inverse).astype(jnp.bfloat16), values_ref[...], preferred_element_type=jnp.float32
    )
    for h in range(heads):
        at = slice(h * HD, (h + 1) * HD)
        out_ref[:, at] = tokens_ref[:, at].astype(jnp.float32) + context[h * rows : (h + 1) * rows]


def attend(tokens, queries, keys_local, values_local, prompt_keys, prompt_values, heads=4):
    rows, width = tokens.shape
    prefix = prompt_keys.shape[0]
    per_key = HEADS // KVH // heads
    wide = pl.BlockSpec((rows, heads * HD), lambda i: (0, i))
    own = pl.BlockSpec((rows, HD), lambda i: (0, i // per_key))
    shared = pl.BlockSpec((prefix, HD), lambda i: (0, i // per_key))
    return pl.pallas_call(
        functools.partial(attend_kernel, heads),
        grid=(HEADS // heads,),
        out_shape=jax.ShapeDtypeStruct((rows, width), jnp.float32),
        in_specs=[wide, own, own, shared, shared, wide],
        out_specs=wide,
        compiler_params=pltpu.CompilerParams(vmem_limit_bytes=24 * 2**20),
        cost_estimate=pl.CostEstimate(
            flops=4 * rows * (prefix + rows) * width,
            bytes_accessed=8 * rows * width,
            transcendentals=rows * (prefix + rows) * HEADS,
        ),
        name="attend",
    )(queries, keys_local, values_local, prompt_keys, prompt_values, tokens)


PLANE = 4
CHUNK = 1024
SUB = 8
SMALL = 16 * 2**20
LARGE = 60 * 2**20


def capacity(tokens, owners):
    return min(tokens, max(2, tokens * TOPK * 4 // (3 * owners)))


def packing(count, width):
    full = count // SUB * SUB
    left = count - full
    pieces = left * (width // CHUNK)
    columns = -(-pieces // (full // SUB)) * LANES
    return full, left, columns


def place_of(piece, full, width):
    high, wide = divmod(piece, full // SUB)
    return slice(wide * SUB, wide * SUB + SUB), slice(width + high * LANES, width + (high + 1) * LANES)


def chunks(width):
    return [slice(at, at + CHUNK) for at in range(0, width, CHUNK)]


def pack(out_ref, rows, at, count, width):
    full, left, _ = packing(count, width)
    out_ref[:, at] = rows[:full].astype(jnp.bfloat16)
    for q in range(left):
        line = rows[full + q : full + q + 1]
        tile = jnp.concatenate([line[:, c : c + LANES] for c in range(0, CHUNK, LANES)], 0)
        piece = q * (width // CHUNK) + at.start // CHUNK
        sub, lane = place_of(piece, full, width)
        out_ref[sub, lane] = tile.astype(jnp.bfloat16)


def unpack(ref, at, count, width):
    full, left, _ = packing(count, width)
    rows = ref[:, at].astype(jnp.float32)
    if not left:
        return rows
    lines = [rows]
    for q in range(left):
        piece = q * (width // CHUNK) + at.start // CHUNK
        sub, lane = place_of(piece, full, width)
        tile = ref[sub, lane].astype(jnp.float32)
        lines.append(jnp.concatenate([tile[c : c + 1] for c in range(SUB)], 1))
    lines.append(jnp.zeros((SUB - left, CHUNK), jnp.float32))
    return jnp.concatenate(lines, 0)


def padded_rows(count):
    return -(-count // SUB) * SUB


def choose(count, slot_ref, base_ref, outs):
    tokens, padded = base_ref.shape
    width = padded // CHUNK * CHUNK
    extra = padded - width
    size = padded_rows(count)
    row = lax.broadcasted_iota(jnp.int32, (tokens, tokens), 0)
    column = lax.broadcasted_iota(jnp.int32, (tokens, tokens), 1)
    turned = lax.dot_general(
        base_ref[:, width:],
        (row == column).astype(jnp.bfloat16),
        (((0,), (0,)), ((), ())),
        preferred_element_type=jnp.float32,
    )
    part = lax.broadcasted_iota(jnp.int32, (extra, tokens), 0)
    routed = [
        jnp.sum(jnp.where(part == (slot_ref[0] ^ j), turned, 0.0), axis=0, keepdims=True) > 0.0
        for j in range(PLANE)
    ]
    ones = jnp.concatenate([r.astype(jnp.float32) for r in routed] * 2, 0).astype(jnp.bfloat16)
    place = jnp.dot(ones, (row < column).astype(jnp.bfloat16), preferred_element_type=jnp.float32)
    target = lax.broadcasted_iota(jnp.int32, (size, tokens), 0)
    chooser = jnp.concatenate(
        [
            jnp.where(
                (target == place[j : j + 1].astype(jnp.int32)) & routed[j], 1.0, 0.0
            ).astype(jnp.bfloat16)
            for j in range(PLANE)
        ],
        0,
    )
    for at in chunks(width):
        rows = jnp.dot(chooser, base_ref[:, at], preferred_element_type=jnp.float32)
        for j in range(PLANE):
            pack(outs[j], rows[j * size : (j + 1) * size], at, count, width)


def clear(outs, count, width):
    full, left, columns = packing(count, width)
    pieces = left * (width // CHUNK)
    for piece in range(pieces, columns // LANES * (full // SUB)):
        sub, lane = place_of(piece, full, width)
        for out in outs:
            out[sub, lane] = jnp.zeros((SUB, LANES), jnp.bfloat16)


def payload_kernel(
    experts, count, slot_ref, holder_ref, tokens_ref, gain_ref, ids_ref, route_ref, out_ref, *outs
):
    rows, width = tokens_ref.shape
    wide = tokens_ref[...].astype(jnp.float32)
    scale = lax.rsqrt(jnp.mean(wide * wide, axis=-1, keepdims=True) + 1e-06)
    out_ref[:, :width] = (wide * scale * gain_ref[...]).astype(jnp.bfloat16)
    extra = out_ref.shape[1] - width
    part = lax.broadcasted_iota(jnp.int32, (extra, rows), 0)
    slot = part % experts
    held = jnp.zeros((extra, rows), jnp.int32)
    for i in range(experts):
        held = jnp.where(slot == i, holder_ref[i], held)
    route = route_ref[...]
    share = route / jnp.sum(route, axis=0, keepdims=True)
    per_slot = jnp.zeros((extra, rows), jnp.float32)
    for k in range(ids_ref.shape[0]):
        per_slot += jnp.where(ids_ref[k : k + 1] == held, share[k : k + 1], 0.0)
    high = per_slot.astype(jnp.bfloat16).astype(jnp.float32)
    both = jnp.where(part < experts, high, jnp.where(part < 2 * experts, per_slot - high, 0.0))
    same = lax.broadcasted_iota(jnp.int32, (rows, rows), 0) == lax.broadcasted_iota(
        jnp.int32, (rows, rows), 1
    )
    turned = lax.dot_general(
        same.astype(jnp.bfloat16),
        both.astype(jnp.bfloat16),
        (((1,), (1,)), ((), ())),
        preferred_element_type=jnp.float32,
    )
    out_ref[:, width:] = turned.astype(jnp.bfloat16)
    choose(count, slot_ref, out_ref, outs)
    clear(outs, count, width)


def packed_shape(count, width):
    full, _, columns = packing(count, width)
    return jax.ShapeDtypeStruct((full, width + columns), jnp.bfloat16)


def make_payload(slot, tokens, norm_gain, expert_ids, route_weight, holder, count):
    rows, width = tokens.shape
    experts = holder.shape[0]
    extra = -(-2 * experts // LANES) * LANES
    vmem = pl.BlockSpec(memory_space=pltpu.VMEM)
    outs = pl.pallas_call(
        functools.partial(payload_kernel, experts, count),
        out_shape=[jax.ShapeDtypeStruct((rows, width + extra), jnp.bfloat16)]
        + [packed_shape(count, width)] * PLANE,
        in_specs=[pl.BlockSpec(memory_space=pltpu.SMEM)] * 2 + [vmem] * 4,
        out_specs=[vmem] * (PLANE + 1),
        compiler_params=pltpu.CompilerParams(vmem_limit_bytes=LARGE),
        name="payload",
    )(slot, holder, tokens, norm_gain.reshape(1, -1), expert_ids.T, route_weight.T)
    return outs[0], outs[1:]


def dispatch_kernel(count, slot_ref, base_ref, *outs):
    choose(count, slot_ref, base_ref, outs)
    clear(outs, count, base_ref.shape[1] // CHUNK * CHUNK)


def dispatch(slot, base, count, width):
    vmem = pl.BlockSpec(memory_space=pltpu.VMEM)
    tokens, padded = base.shape
    return pl.pallas_call(
        functools.partial(dispatch_kernel, count),
        out_shape=[packed_shape(count, width)] * PLANE,
        in_specs=[pl.BlockSpec(memory_space=pltpu.SMEM), vmem],
        out_specs=[vmem] * PLANE,
        cost_estimate=pl.CostEstimate(
            flops=2 * PLANE * count * tokens * padded,
            bytes_accessed=2 * (tokens + PLANE * count) * padded,
            transcendentals=0,
        ),
        compiler_params=pltpu.CompilerParams(vmem_limit_bytes=SMALL),
        name="dispatch",
    )(slot, base)


def combine_kernel(extras, experts, count, slot_ref, meta_ref, *refs):
    results, terms, out_ref = refs[:PLANE], refs[PLANE : PLANE + extras], refs[-1]
    tokens, extra = meta_ref.shape
    width = out_ref.shape[1]
    size = padded_rows(count)
    row = lax.broadcasted_iota(jnp.int32, (tokens, tokens), 0)
    column = lax.broadcasted_iota(jnp.int32, (tokens, tokens), 1)
    lane = lax.broadcasted_iota(jnp.int32, (tokens, extra), 1)
    meta = meta_ref[...].astype(jnp.float32)
    before = (column < row).astype(jnp.bfloat16)
    target = lax.broadcasted_iota(jnp.int32, (tokens, size), 1)
    chooser, shares = [], []
    for j in range(PLANE):
        at_slot = lane == (slot_ref[0] ^ j)
        high = jnp.sum(jnp.where(at_slot, meta, 0.0), axis=1, keepdims=True)
        routed = high > 0.0
        ones = jnp.broadcast_to(jnp.where(routed, 1.0, 0.0), (tokens, size)).astype(jnp.bfloat16)
        place = jnp.dot(before, ones, preferred_element_type=jnp.float32)
        mine = jnp.where((target == place.astype(jnp.int32)) & routed, 1.0, 0.0)
        mine = mine.astype(jnp.bfloat16)
        both = jnp.where(at_slot | (lane == (slot_ref[0] ^ j) + experts), meta, 0.0)
        per_row = lax.dot_general(
            mine,
            both.astype(jnp.bfloat16),
            (((0,), (0,)), ((), ())),
            preferred_element_type=jnp.float32,
        )
        shares.append(jnp.sum(per_row, axis=1, keepdims=True))
        chooser.append(mine)
    chooser = jnp.concatenate(chooser, 1)
    shares = jnp.concatenate(shares, 0)
    for at in chunks(width):
        rows = jnp.concatenate([unpack(r, at, count, width) for r in results], 0)
        rows = (rows * shares).astype(jnp.bfloat16)
        total = jnp.dot(chooser, rows, preferred_element_type=jnp.float32)
        for term in terms:
            total = total + term[:, at].astype(jnp.float32)
        out_ref[:, at] = total.astype(out_ref.dtype)


def combine(slot, base, results, terms, dtype, experts, count, width):
    tokens, padded = base.shape
    extra = padded - width
    whole = lambda a: pl.BlockSpec(a.shape, lambda i: (0, 0))
    return pl.pallas_call(
        functools.partial(combine_kernel, len(terms), experts, count),
        grid=(1,),
        out_shape=jax.ShapeDtypeStruct((tokens, width), dtype),
        in_specs=[
            pl.BlockSpec(memory_space=pltpu.SMEM),
            pl.BlockSpec((tokens, extra), lambda i: (0, width // extra)),
        ]
        + [whole(a) for a in (*results, *terms)],
        out_specs=pl.BlockSpec((tokens, width), lambda i: (0, 0)),
        cost_estimate=pl.CostEstimate(
            flops=2 * PLANE * count * tokens * width,
            bytes_accessed=2 * (tokens + PLANE * count) * width,
            transcendentals=0,
        ),
        compiler_params=pltpu.CompilerParams(vmem_limit_bytes=SMALL),
        name="combine",
    )(slot, base, *results, *terms)


def ffn_kernel(count, *refs):
    blocks, refs = refs[:PLANE], refs[PLANE:]
    gate_m, up_m, down_m, gate_p, up_p, down_p = refs[:6]
    outs, (rows_buf, hid_buf) = refs[6 : 6 + PLANE], refs[6 + PLANE :]
    width, half = gate_m.shape
    size = padded_rows(count)
    for at in chunks(width):
        for i, block in enumerate(blocks):
            rows = unpack(block, at, count, width)
            rows_buf[i * size : (i + 1) * size, at] = rows.astype(jnp.bfloat16)
    for side, (gate_w, up_w) in enumerate(((gate_m, up_m), (gate_p, up_p))):
        gate = jnp.dot(rows_buf[...], gate_w[...], preferred_element_type=jnp.float32)
        up = jnp.dot(rows_buf[...], up_w[...], preferred_element_type=jnp.float32)
        hid_buf[:, side * half : (side + 1) * half] = (
            gate / (1.0 + jnp.exp(-gate)) * up
        ).astype(jnp.bfloat16)
    for at in chunks(width):
        result = jnp.dot(hid_buf[:, :half], down_m[:, at], preferred_element_type=jnp.float32)
        result += jnp.dot(hid_buf[:, half:], down_p[:, at], preferred_element_type=jnp.float32)
        for i in range(PLANE):
            pack(outs[i], result[i * size : (i + 1) * size], at, count, width)
    clear(outs, count, width)


def run_ffn(blocks, weights, count):
    rows = PLANE * padded_rows(count)
    width, half = weights[0].shape
    vmem = pl.BlockSpec(memory_space=pltpu.VMEM)
    return pl.pallas_call(
        functools.partial(ffn_kernel, count),
        out_shape=[packed_shape(count, width)] * PLANE,
        in_specs=[vmem] * (PLANE + 6),
        out_specs=[vmem] * PLANE,
        scratch_shapes=[
            pltpu.VMEM((rows, width), jnp.bfloat16),
            pltpu.VMEM((rows, 2 * half), jnp.bfloat16),
        ],
        compiler_params=pltpu.CompilerParams(vmem_limit_bytes=SMALL),
        cost_estimate=pl.CostEstimate(
            flops=2 * rows * width * half * 6,
            bytes_accessed=12 * width * half + 4 * rows * width,
            transcendentals=rows * half * 2,
        ),
        name="ffn",
    )(*blocks, *weights)


def after(value, *others):
    return lax.optimization_barrier((value,) + others)[0]


def local(
    tokens,
    queries,
    keys_local,
    values_local,
    prompt_keys,
    prompt_values,
    norm_gain,
    expert_ids,
    route_weight,
    stored_gate,
    stored_up,
    stored_down,
    holder,
):
    owners = lax.axis_size("expert")
    experts = holder.shape[0]
    columns = owners // 4
    f32, bf16 = jnp.float32, jnp.bfloat16

    def swap(value, offset):
        return lax.ppermute(value, "expert", [(i, i ^ offset) for i in range(owners)])

    def partner(value):
        return lax.ppermute(value, "dp", [(0, 1), (1, 0)])

    own_weights = (stored_gate[0], stored_up[0], stored_down[0])
    weights = own_weights + tuple(partner(w) for w in own_weights)
    slot = lax.axis_index("expert").astype(jnp.int32).reshape(1)
    width = tokens.shape[1]
    count = capacity(tokens.shape[0], owners)
    payload, chosen = make_payload(slot, tokens, norm_gain, expert_ids, route_weight, holder, count)
    bases, blocks, outs = {}, {}, {}

    def gather(k, base, ready=None):
        bases[k] = base
        if ready is None:
            ready = dispatch(slot, base, count, width)
        own, to_x, to_y, to_d = ready
        blocks[k] = (own, swap(to_x, 1), swap(to_y, 2), swap(to_d, 3))

    def serve(k):
        own, to_x, to_y, to_d = run_ffn(blocks[k], weights, count)
        outs[k] = (own, swap(to_x, 1), swap(to_y, 2), swap(to_d, 3))

    def collect(k, terms=(), dtype=bf16):
        return combine(slot, bases[k], outs[k], terms, dtype, experts, count, width)

    gather(0, payload, chosen)
    result = attend(tokens, queries, keys_local, values_local, prompt_keys, prompt_values)
    for first in range(0, columns, 4):
        if first == 0:
            gather(1, swap(payload, 4))
            gather(2, swap(after(payload, bases[1]), 8))
        else:
            gather(first, swap(payload, 4 * first))
            gather(first + 1, swap(payload, 4 * first + 4))
            gather(first + 2, swap(payload, 4 * first + 8))
        gather(first + 3, swap(bases[first + 2], 4))
    for k in range(columns):
        serve(k)
    sums = []
    for k in range(1, columns):
        sums.append(swap(collect(k), 4 * k))
    result = collect(0, (result,), f32)
    for part in sums:
        result = result + part.astype(f32)
    return result.astype(bf16)


def solution(mesh):
    return jax.shard_map(
        local,
        mesh=mesh,
        in_specs=(
            P(("group", "expert", "dp"), None),
            P(("group", "expert", "dp"), None),
            P(("group", "expert", "dp"), None),
            P(("group", "expert", "dp"), None),
            P("group", None),
            P("group", None),
            P(),
            P(("group", "expert", "dp"), None),
            P(("group", "expert", "dp"), None),
            P("expert", None, "dp"),
            P("expert", None, "dp"),
            P("expert", "dp", None),
            P(),
        ),
        out_specs=P(("group", "expert", "dp"), None),
        check_vma=False,
    )
```

```python
import functools

import jax
import jax.numpy as jnp
from jax import lax
from jax.experimental import pallas as pl
from jax.experimental.pallas import tpu as pltpu
from jax.sharding import PartitionSpec as P


HEADS = 32
KVH = 2
HD = 128
TOPK = 8
LANES = 128


def attend_kernel(heads, q_ref, keys_ref, values_ref, pkeys_ref, pvalues_ref, tokens_ref, out_ref):
    rows = q_ref.shape[0]
    dims = (((1,), (1,)), ((), ()))
    scale = HD ** (-0.5)
    stacked = jnp.concatenate([q_ref[:, h * HD : (h + 1) * HD] for h in range(heads)], 0)
    first = lax.dot_general(stacked, pkeys_ref[...], dims, preferred_element_type=jnp.float32)
    last = lax.dot_general(stacked, keys_ref[...], dims, preferred_element_type=jnp.float32)
    query = lax.broadcasted_iota(jnp.int32, (rows, rows), 0)
    key = lax.broadcasted_iota(jnp.int32, (rows, rows), 1)
    allowed = jnp.concatenate([key <= query] * heads, 0)
    first = first * scale
    last = jnp.where(allowed, last * scale, -jnp.inf)
    highest = jnp.maximum(
        jnp.max(first, axis=-1, keepdims=True), jnp.max(last, axis=-1, keepdims=True)
    )
    first, last = jnp.exp(first - highest), jnp.exp(last - highest)
    total = jnp.sum(first, axis=-1, keepdims=True) + jnp.sum(last, axis=-1, keepdims=True)
    inverse = 1.0 / total
    context = jnp.dot(
        (first * inverse).astype(jnp.bfloat16), pvalues_ref[...], preferred_element_type=jnp.float32
    ) + jnp.dot(
        (last * inverse).astype(jnp.bfloat16), values_ref[...], preferred_element_type=jnp.float32
    )
    for h in range(heads):
        at = slice(h * HD, (h + 1) * HD)
        out_ref[:, at] = tokens_ref[:, at].astype(jnp.float32) + context[h * rows : (h + 1) * rows]


def attend(part, tokens, queries, keys_local, values_local, prompt_keys, prompt_values, heads=4):
    rows, width = tokens.shape[0], tokens.shape[1] // KVH
    prefix = prompt_keys.shape[0]
    steps = HEADS // KVH // heads
    wide = pl.BlockSpec((rows, heads * HD), lambda i: (0, part * steps + i))
    own = pl.BlockSpec((rows, HD), lambda i: (0, part))
    shared = pl.BlockSpec((prefix, HD), lambda i: (0, part))
    return pl.pallas_call(
        functools.partial(attend_kernel, heads),
        grid=(steps,),
        out_shape=jax.ShapeDtypeStruct((rows, width), jnp.float32),
        in_specs=[wide, own, own, shared, shared, wide],
        out_specs=pl.BlockSpec((rows, heads * HD), lambda i: (0, i)),
        compiler_params=pltpu.CompilerParams(vmem_limit_bytes=24 * 2**20),
        cost_estimate=pl.CostEstimate(
            flops=4 * rows * (prefix + rows) * width,
            bytes_accessed=8 * rows * width,
            transcendentals=rows * (prefix + rows) * HEADS // KVH,
        ),
        name="attend",
    )(*[
        pltpu.with_memory_space_constraint(a, pltpu.HBM)
        for a in (queries, keys_local, values_local, prompt_keys, prompt_values, tokens)
    ])


PLANE = 4
CHUNK = 1024
SUB = 8
SMALL = 16 * 2**20
LARGE = 60 * 2**20


def capacity(tokens, owners):
    return min(tokens, max(2, tokens * TOPK * 4 // (3 * owners)))


def packing(count, width):
    full = count // SUB * SUB
    left = count - full
    pieces = left * (width // CHUNK)
    columns = -(-pieces // (full // SUB)) * LANES
    return full, left, columns


def place_of(piece, full, width):
    high, wide = divmod(piece, full // SUB)
    return slice(wide * SUB, wide * SUB + SUB), slice(width + high * LANES, width + (high + 1) * LANES)


def chunks(width):
    return [slice(at, at + CHUNK) for at in range(0, width, CHUNK)]


def pack(out_ref, rows, at, count, width):
    full, left, _ = packing(count, width)
    out_ref[:, at] = rows[:full].astype(jnp.bfloat16)
    for q in range(left):
        line = rows[full + q : full + q + 1]
        tile = jnp.concatenate([line[:, c : c + LANES] for c in range(0, CHUNK, LANES)], 0)
        piece = q * (width // CHUNK) + at.start // CHUNK
        sub, lane = place_of(piece, full, width)
        out_ref[sub, lane] = tile.astype(jnp.bfloat16)


def unpack(ref, at, count, width):
    full, left, _ = packing(count, width)
    rows = ref[:, at].astype(jnp.float32)
    if not left:
        return rows
    lines = [rows]
    for q in range(left):
        piece = q * (width // CHUNK) + at.start // CHUNK
        sub, lane = place_of(piece, full, width)
        tile = ref[sub, lane].astype(jnp.float32)
        lines.append(jnp.concatenate([tile[c : c + 1] for c in range(SUB)], 1))
    lines.append(jnp.zeros((SUB - left, CHUNK), jnp.float32))
    return jnp.concatenate(lines, 0)


def padded_rows(count):
    return -(-count // SUB) * SUB


def normed(tokens_ref, gain_ref):
    wide = tokens_ref[...].astype(jnp.float32)
    scale = lax.rsqrt(jnp.mean(wide * wide, axis=-1, keepdims=True) + 1e-06)
    return (wide * scale * gain_ref[...]).astype(jnp.bfloat16)


def choose(count, slot_ref, base_ref, meta, outs):
    tokens, extra = meta.shape
    width = base_ref.shape[1] // CHUNK * CHUNK
    size = padded_rows(count)
    row = lax.broadcasted_iota(jnp.int32, (tokens, tokens), 0)
    column = lax.broadcasted_iota(jnp.int32, (tokens, tokens), 1)
    turned = lax.dot_general(
        meta,
        (row == column).astype(jnp.bfloat16),
        (((0,), (0,)), ((), ())),
        preferred_element_type=jnp.float32,
    )
    part = lax.broadcasted_iota(jnp.int32, (extra, tokens), 0)
    routed = [
        jnp.sum(jnp.where(part == (slot_ref[0] ^ j), turned, 0.0), axis=0, keepdims=True) > 0.0
        for j in range(PLANE)
    ]
    ones = jnp.concatenate([r.astype(jnp.float32) for r in routed] * 2, 0).astype(jnp.bfloat16)
    place = jnp.dot(ones, (row < column).astype(jnp.bfloat16), preferred_element_type=jnp.float32)
    target = lax.broadcasted_iota(jnp.int32, (size, tokens), 0)
    chooser = jnp.concatenate(
        [
            jnp.where(
                (target == place[j : j + 1].astype(jnp.int32)) & routed[j], 1.0, 0.0
            ).astype(jnp.bfloat16)
            for j in range(PLANE)
        ],
        0,
    )
    for at in chunks(width):
        rows = jnp.dot(chooser, base_ref[:, at], preferred_element_type=jnp.float32)
        for j in range(PLANE):
            pack(outs[j], rows[j * size : (j + 1) * size], at, count, width)


def clear(outs, count, width):
    full, left, columns = packing(count, width)
    pieces = left * (width // CHUNK)
    for piece in range(pieces, columns // LANES * (full // SUB)):
        sub, lane = place_of(piece, full, width)
        for out in outs:
            out[sub, lane] = jnp.zeros((SUB, LANES), jnp.bfloat16)


def payload_kernel(
    experts,
    count,
    slot_ref,
    holder_ref,
    tokens_ref,
    gain_ref,
    ids_ref,
    route_ref,
    out_ref,
    meta_ref,
    *outs,
):
    rows, width = tokens_ref.shape
    out_ref[:, :width] = normed(tokens_ref, gain_ref)
    extra = out_ref.shape[1] - width
    part = lax.broadcasted_iota(jnp.int32, (extra, rows), 0)
    slot = part % experts
    held = jnp.zeros((extra, rows), jnp.int32)
    for i in range(experts):
        held = jnp.where(slot == i, holder_ref[i], held)
    route = route_ref[...]
    share = route / jnp.sum(route, axis=0, keepdims=True)
    per_slot = jnp.zeros((extra, rows), jnp.float32)
    for k in range(ids_ref.shape[0]):
        per_slot += jnp.where(ids_ref[k : k + 1] == held, share[k : k + 1], 0.0)
    high = per_slot.astype(jnp.bfloat16).astype(jnp.float32)
    both = jnp.where(part < experts, high, jnp.where(part < 2 * experts, per_slot - high, 0.0))
    same = lax.broadcasted_iota(jnp.int32, (rows, rows), 0) == lax.broadcasted_iota(
        jnp.int32, (rows, rows), 1
    )
    turned = lax.dot_general(
        same.astype(jnp.bfloat16),
        both.astype(jnp.bfloat16),
        (((1,), (1,)), ((), ())),
        preferred_element_type=jnp.float32,
    )
    meta = turned.astype(jnp.bfloat16)
    out_ref[:, width:] = meta
    meta_ref[...] = meta
    choose(count, slot_ref, out_ref, meta, outs)
    clear(outs, count, width)


def packed_shape(count, width):
    full, _, columns = packing(count, width)
    return jax.ShapeDtypeStruct((full, width + columns), jnp.bfloat16)


def make_payload(slot, tokens, norm_gain, expert_ids, route_weight, holder, count):
    rows, width = tokens.shape
    experts = holder.shape[0]
    extra = -(-2 * experts // LANES) * LANES
    vmem = pl.BlockSpec(memory_space=pltpu.VMEM)
    outs = pl.pallas_call(
        functools.partial(payload_kernel, experts, count),
        out_shape=[
            jax.ShapeDtypeStruct((rows, width + extra), jnp.bfloat16),
            jax.ShapeDtypeStruct((rows, extra), jnp.bfloat16),
        ]
        + [packed_shape(count, width)] * PLANE,
        in_specs=[pl.BlockSpec(memory_space=pltpu.SMEM)] * 2 + [vmem] * 4,
        out_specs=[vmem] * (PLANE + 2),
        compiler_params=pltpu.CompilerParams(vmem_limit_bytes=LARGE),
        name="payload",
    )(slot, holder, tokens, norm_gain.reshape(1, -1), expert_ids.T, route_weight.T)
    return outs[0], outs[1], outs[2:]


def dispatch_kernel(count, slot_ref, base_ref, *outs):
    width = base_ref.shape[1] // CHUNK * CHUNK
    choose(count, slot_ref, base_ref, base_ref[:, width:], outs)
    clear(outs, count, width)


def raw_dispatch_kernel(count, slot_ref, tokens_ref, meta_ref, gain_ref, *refs):
    outs, rows_buf = refs[:PLANE], refs[PLANE]
    rows_buf[...] = normed(tokens_ref, gain_ref)
    choose(count, slot_ref, rows_buf, meta_ref[...], outs)
    clear(outs, count, tokens_ref.shape[1])


def dispatch(slot, base, count, width):
    vmem = pl.BlockSpec(memory_space=pltpu.VMEM)
    raw = isinstance(base, tuple)
    operands = base if raw else (base,)
    tokens = operands[0].shape[0]
    return pl.pallas_call(
        functools.partial(raw_dispatch_kernel if raw else dispatch_kernel, count),
        out_shape=[packed_shape(count, width)] * PLANE,
        in_specs=[pl.BlockSpec(memory_space=pltpu.SMEM)] + [vmem] * len(operands),
        out_specs=[vmem] * PLANE,
        scratch_shapes=[pltpu.VMEM((tokens, width), jnp.bfloat16)] if raw else [],
        cost_estimate=pl.CostEstimate(
            flops=2 * PLANE * count * tokens * width,
            bytes_accessed=2 * (tokens + PLANE * count) * width,
            transcendentals=0,
        ),
        compiler_params=pltpu.CompilerParams(vmem_limit_bytes=SMALL),
        name="dispatch",
    )(slot, *operands)


def combine_kernel(extras, experts, count, slot_ref, meta_ref, *refs):
    results, terms, out_ref = refs[:PLANE], refs[PLANE : PLANE + extras], refs[-1]
    tokens, extra = meta_ref.shape
    width = out_ref.shape[1]
    size = padded_rows(count)
    row = lax.broadcasted_iota(jnp.int32, (tokens, tokens), 0)
    column = lax.broadcasted_iota(jnp.int32, (tokens, tokens), 1)
    lane = lax.broadcasted_iota(jnp.int32, (tokens, extra), 1)
    meta = meta_ref[...].astype(jnp.float32)
    before = (column < row).astype(jnp.bfloat16)
    target = lax.broadcasted_iota(jnp.int32, (tokens, size), 1)
    chooser, shares = [], []
    for j in range(PLANE):
        at_slot = lane == (slot_ref[0] ^ j)
        high = jnp.sum(jnp.where(at_slot, meta, 0.0), axis=1, keepdims=True)
        routed = high > 0.0
        ones = jnp.broadcast_to(jnp.where(routed, 1.0, 0.0), (tokens, size)).astype(jnp.bfloat16)
        place = jnp.dot(before, ones, preferred_element_type=jnp.float32)
        mine = jnp.where((target == place.astype(jnp.int32)) & routed, 1.0, 0.0)
        mine = mine.astype(jnp.bfloat16)
        both = jnp.where(at_slot | (lane == (slot_ref[0] ^ j) + experts), meta, 0.0)
        per_row = lax.dot_general(
            mine,
            both.astype(jnp.bfloat16),
            (((0,), (0,)), ((), ())),
            preferred_element_type=jnp.float32,
        )
        shares.append(jnp.sum(per_row, axis=1, keepdims=True))
        chooser.append(mine)
    chooser = jnp.concatenate(chooser, 1)
    shares = jnp.concatenate(shares, 0)
    for at in chunks(width):
        rows = jnp.concatenate([unpack(r, at, count, width) for r in results], 0)
        rows = (rows * shares).astype(jnp.bfloat16)
        total = jnp.dot(chooser, rows, preferred_element_type=jnp.float32)
        if terms:
            part, start = divmod(at.start, width // len(terms))
            total = total + terms[part][:, start : start + CHUNK].astype(jnp.float32)
        out_ref[:, at] = total.astype(out_ref.dtype)


def combine(slot, base, results, terms, dtype, experts, count, width):
    tokens, padded = base.shape
    extra = padded % CHUNK
    whole = lambda a: pl.BlockSpec(a.shape, lambda i: (0, 0))
    return pl.pallas_call(
        functools.partial(combine_kernel, len(terms), experts, count),
        grid=(1,),
        out_shape=jax.ShapeDtypeStruct((tokens, width), dtype),
        in_specs=[
            pl.BlockSpec(memory_space=pltpu.SMEM),
            pl.BlockSpec((tokens, extra), lambda i: (0, padded // extra - 1)),
        ]
        + [whole(a) for a in (*results, *terms)],
        out_specs=pl.BlockSpec((tokens, width), lambda i: (0, 0)),
        cost_estimate=pl.CostEstimate(
            flops=2 * PLANE * count * tokens * width,
            bytes_accessed=2 * (tokens + PLANE * count) * width,
            transcendentals=0,
        ),
        compiler_params=pltpu.CompilerParams(vmem_limit_bytes=SMALL),
        name="combine",
    )(slot, base, *results, *terms)


def ffn_kernel(count, *refs):
    blocks, refs = refs[:PLANE], refs[PLANE:]
    gate_m, up_m, down_m, gate_p, up_p, down_p = refs[:6]
    outs, (rows_buf, hid_buf) = refs[6 : 6 + PLANE], refs[6 + PLANE :]
    width, half = gate_m.shape
    size = padded_rows(count)
    for at in chunks(width):
        for i, block in enumerate(blocks):
            rows = unpack(block, at, count, width)
            rows_buf[i * size : (i + 1) * size, at] = rows.astype(jnp.bfloat16)
    for side, (gate_w, up_w) in enumerate(((gate_m, up_m), (gate_p, up_p))):
        gate = jnp.dot(rows_buf[...], gate_w[...], preferred_element_type=jnp.float32)
        up = jnp.dot(rows_buf[...], up_w[...], preferred_element_type=jnp.float32)
        hid_buf[:, side * half : (side + 1) * half] = (
            gate / (1.0 + jnp.exp(-gate)) * up
        ).astype(jnp.bfloat16)
    for at in chunks(width):
        result = jnp.dot(hid_buf[:, :half], down_m[:, at], preferred_element_type=jnp.float32)
        result += jnp.dot(hid_buf[:, half:], down_p[:, at], preferred_element_type=jnp.float32)
        for i in range(PLANE):
            pack(outs[i], result[i * size : (i + 1) * size], at, count, width)
    clear(outs, count, width)


def run_ffn(blocks, weights, count):
    rows = PLANE * padded_rows(count)
    width, half = weights[0].shape
    vmem = pl.BlockSpec(memory_space=pltpu.VMEM)
    return pl.pallas_call(
        functools.partial(ffn_kernel, count),
        out_shape=[packed_shape(count, width)] * PLANE,
        in_specs=[vmem] * (PLANE + 6),
        out_specs=[vmem] * PLANE,
        scratch_shapes=[
            pltpu.VMEM((rows, width), jnp.bfloat16),
            pltpu.VMEM((rows, 2 * half), jnp.bfloat16),
        ],
        compiler_params=pltpu.CompilerParams(vmem_limit_bytes=SMALL),
        cost_estimate=pl.CostEstimate(
            flops=2 * rows * width * half * 6,
            bytes_accessed=12 * width * half + 4 * rows * width,
            transcendentals=rows * half * 2,
        ),
        name="ffn",
    )(*blocks, *weights)


def local(
    tokens,
    queries,
    keys_local,
    values_local,
    prompt_keys,
    prompt_values,
    norm_gain,
    expert_ids,
    route_weight,
    stored_gate,
    stored_up,
    stored_down,
    holder,
):
    owners = lax.axis_size("expert")
    experts = holder.shape[0]
    columns = owners // 4
    f32, bf16 = jnp.float32, jnp.bfloat16

    def swap(value, offset):
        return lax.ppermute(value, "expert", [(i, i ^ offset) for i in range(owners)])

    def partner(value):
        return lax.ppermute(value, "dp", [(0, 1), (1, 0)])

    own_weights = (stored_gate[0], stored_up[0], stored_down[0])
    weights = own_weights + tuple(partner(w) for w in own_weights)
    slot = lax.axis_index("expert").astype(jnp.int32).reshape(1)
    width = tokens.shape[1]
    count = capacity(tokens.shape[0], owners)
    payload, meta, chosen = make_payload(
        slot, tokens, norm_gain, expert_ids, route_weight, holder, count
    )
    bases, blocks, outs = {}, {}, {}

    def gather(k, base, ready=None):
        bases[k] = base
        if ready is None:
            ready = dispatch(slot, base, count, width)
        own, to_x, to_y, to_d = ready
        blocks[k] = (own, swap(to_x, 1), swap(to_y, 2), swap(to_d, 3))

    def serve(k):
        own, to_x, to_y, to_d = run_ffn(blocks[k], weights, count)
        outs[k] = (own, swap(to_x, 1), swap(to_y, 2), swap(to_d, 3))

    def collect(k, terms=(), dtype=bf16):
        return combine(slot, bases[k], outs[k], terms, dtype, experts, count, width)

    gather(0, payload, chosen)
    result = []
    for part in range(KVH):
        result.append(
            attend(
                part, tokens, queries, keys_local, values_local, prompt_keys, prompt_values
            )
        )
    for first in range(0, columns, 4):
        if first == 0:
            lanes = swap(meta, 4)
            gather(1, (swap(tokens, 4), lanes, norm_gain.reshape(1, -1)))
            bases[1] = lanes
            gather(2, swap(payload, 8))
        else:
            gather(first, swap(payload, 4 * first))
            gather(first + 1, swap(payload, 4 * first + 4))
            gather(first + 2, swap(payload, 4 * first + 8))
        gather(first + 3, swap(bases[first + 2], 4))
    for k in range(columns):
        serve(k)
    sums = []
    for k in range(1, columns):
        sums.append(swap(collect(k), 4 * k))
    result = collect(0, result, f32)
    for part in sums:
        result = result + part.astype(f32)
    return result.astype(bf16)


def solution(mesh):
    return jax.shard_map(
        local,
        mesh=mesh,
        in_specs=(
            P(("group", "expert", "dp"), None),
            P(("group", "expert", "dp"), None),
            P(("group", "expert", "dp"), None),
            P(("group", "expert", "dp"), None),
            P("group", None),
            P("group", None),
            P(),
            P(("group", "expert", "dp"), None),
            P(("group", "expert", "dp"), None),
            P("expert", None, "dp"),
            P("expert", None, "dp"),
            P("expert", "dp", None),
            P(),
        ),
        out_specs=P(("group", "expert", "dp"), None),
        check_vma=False,
    )
```

```python
import functools

import jax
import jax.numpy as jnp
from jax import lax
from jax.experimental import pallas as pl
from jax.experimental.pallas import tpu as pltpu
from jax.sharding import PartitionSpec as P


HEADS = 32
KVH = 2
HD = 128
TOPK = 8
LANES = 128


def attend_kernel(heads, q_ref, keys_ref, values_ref, pkeys_ref, pvalues_ref, tokens_ref, out_ref):
    rows = q_ref.shape[0]
    dims = (((1,), (1,)), ((), ()))
    scale = HD ** (-0.5)
    stacked = jnp.concatenate([q_ref[:, h * HD : (h + 1) * HD] for h in range(heads)], 0)
    first = lax.dot_general(stacked, pkeys_ref[...], dims, preferred_element_type=jnp.float32)
    last = lax.dot_general(stacked, keys_ref[...], dims, preferred_element_type=jnp.float32)
    query = lax.broadcasted_iota(jnp.int32, (rows, rows), 0)
    key = lax.broadcasted_iota(jnp.int32, (rows, rows), 1)
    allowed = jnp.concatenate([key <= query] * heads, 0)
    first = first * scale
    last = jnp.where(allowed, last * scale, -jnp.inf)
    highest = jnp.maximum(
        jnp.max(first, axis=-1, keepdims=True), jnp.max(last, axis=-1, keepdims=True)
    )
    first, last = jnp.exp(first - highest), jnp.exp(last - highest)
    total = jnp.sum(first, axis=-1, keepdims=True) + jnp.sum(last, axis=-1, keepdims=True)
    inverse = 1.0 / total
    context = jnp.dot(
        (first * inverse).astype(jnp.bfloat16), pvalues_ref[...], preferred_element_type=jnp.float32
    ) + jnp.dot(
        (last * inverse).astype(jnp.bfloat16), values_ref[...], preferred_element_type=jnp.float32
    )
    for h in range(heads):
        at = slice(h * HD, (h + 1) * HD)
        out_ref[:, at] = tokens_ref[:, at].astype(jnp.float32) + context[h * rows : (h + 1) * rows]


def attend(part, tokens, queries, keys_local, values_local, prompt_keys, prompt_values, heads=4):
    rows, width = tokens.shape[0], tokens.shape[1] // KVH
    prefix = prompt_keys.shape[0]
    steps = HEADS // KVH // heads
    wide = pl.BlockSpec((rows, heads * HD), lambda i: (0, part * steps + i))
    own = pl.BlockSpec((rows, HD), lambda i: (0, part))
    shared = pl.BlockSpec((prefix, HD), lambda i: (0, part))
    return pl.pallas_call(
        functools.partial(attend_kernel, heads),
        grid=(steps,),
        out_shape=jax.ShapeDtypeStruct((rows, width), jnp.float32),
        in_specs=[wide, own, own, shared, shared, wide],
        out_specs=pl.BlockSpec((rows, heads * HD), lambda i: (0, i)),
        compiler_params=pltpu.CompilerParams(vmem_limit_bytes=24 * 2**20),
        cost_estimate=pl.CostEstimate(
            flops=4 * rows * (prefix + rows) * width,
            bytes_accessed=8 * rows * width,
            transcendentals=rows * (prefix + rows) * HEADS // KVH,
        ),
        name="attend",
    )(*[
        pltpu.with_memory_space_constraint(a, pltpu.HBM)
        for a in (queries, keys_local, values_local, prompt_keys, prompt_values, tokens)
    ])


PLANE = 4
CHUNK = 1024
SUB = 8
SMALL = 16 * 2**20
LARGE = 60 * 2**20


def capacity(tokens, owners):
    return min(tokens, max(2, tokens * TOPK * 4 // (3 * owners)))


def packing(count, width):
    full = count // SUB * SUB
    left = count - full
    pieces = left * (width // CHUNK)
    columns = -(-pieces // (full // SUB)) * LANES
    return full, left, columns


def place_of(piece, full, width):
    high, wide = divmod(piece, full // SUB)
    return slice(wide * SUB, wide * SUB + SUB), slice(width + high * LANES, width + (high + 1) * LANES)


def chunks(width):
    return [slice(at, at + CHUNK) for at in range(0, width, CHUNK)]


def pack(out_ref, rows, at, count, width):
    full, left, _ = packing(count, width)
    out_ref[:, at] = rows[:full].astype(jnp.bfloat16)
    for q in range(left):
        line = rows[full + q : full + q + 1]
        tile = jnp.concatenate([line[:, c : c + LANES] for c in range(0, CHUNK, LANES)], 0)
        piece = q * (width // CHUNK) + at.start // CHUNK
        sub, lane = place_of(piece, full, width)
        out_ref[sub, lane] = tile.astype(jnp.bfloat16)


def unpack(ref, at, count, width):
    full, left, _ = packing(count, width)
    rows = ref[:, at].astype(jnp.float32)
    if not left:
        return rows
    lines = [rows]
    for q in range(left):
        piece = q * (width // CHUNK) + at.start // CHUNK
        sub, lane = place_of(piece, full, width)
        tile = ref[sub, lane].astype(jnp.float32)
        lines.append(jnp.concatenate([tile[c : c + 1] for c in range(SUB)], 1))
    lines.append(jnp.zeros((SUB - left, CHUNK), jnp.float32))
    return jnp.concatenate(lines, 0)


def padded_rows(count):
    return -(-count // SUB) * SUB


def normed(tokens_ref, gain_ref):
    wide = tokens_ref[...].astype(jnp.float32)
    scale = lax.rsqrt(jnp.mean(wide * wide, axis=-1, keepdims=True) + 1e-06)
    return (wide * scale * gain_ref[...]).astype(jnp.bfloat16)


def choose(count, slot_ref, base_ref, meta, outs):
    tokens, extra = meta.shape
    width = base_ref.shape[1] // CHUNK * CHUNK
    size = padded_rows(count)
    row = lax.broadcasted_iota(jnp.int32, (tokens, tokens), 0)
    column = lax.broadcasted_iota(jnp.int32, (tokens, tokens), 1)
    turned = lax.dot_general(
        meta,
        (row == column).astype(jnp.bfloat16),
        (((0,), (0,)), ((), ())),
        preferred_element_type=jnp.float32,
    )
    part = lax.broadcasted_iota(jnp.int32, (extra, tokens), 0)
    routed = [
        jnp.sum(jnp.where(part == (slot_ref[0] ^ j), turned, 0.0), axis=0, keepdims=True) > 0.0
        for j in range(PLANE)
    ]
    ones = jnp.concatenate([r.astype(jnp.float32) for r in routed] * 2, 0).astype(jnp.bfloat16)
    place = jnp.dot(ones, (row < column).astype(jnp.bfloat16), preferred_element_type=jnp.float32)
    target = lax.broadcasted_iota(jnp.int32, (size, tokens), 0)
    chooser = jnp.concatenate(
        [
            jnp.where(
                (target == place[j : j + 1].astype(jnp.int32)) & routed[j], 1.0, 0.0
            ).astype(jnp.bfloat16)
            for j in range(PLANE)
        ],
        0,
    )
    for at in chunks(width):
        rows = jnp.dot(chooser, base_ref[:, at], preferred_element_type=jnp.float32)
        for j in range(PLANE):
            pack(outs[j], rows[j * size : (j + 1) * size], at, count, width)


def clear(outs, count, width):
    full, left, columns = packing(count, width)
    pieces = left * (width // CHUNK)
    for piece in range(pieces, columns // LANES * (full // SUB)):
        sub, lane = place_of(piece, full, width)
        for out in outs:
            out[sub, lane] = jnp.zeros((SUB, LANES), jnp.bfloat16)


def payload_kernel(
    experts,
    count,
    slot_ref,
    holder_ref,
    tokens_ref,
    gain_ref,
    ids_ref,
    route_ref,
    out_ref,
    meta_ref,
    *outs,
):
    rows, width = tokens_ref.shape
    out_ref[:, :width] = normed(tokens_ref, gain_ref)
    extra = out_ref.shape[1] - width
    part = lax.broadcasted_iota(jnp.int32, (extra, rows), 0)
    slot = part % experts
    held = jnp.zeros((extra, rows), jnp.int32)
    for i in range(experts):
        held = jnp.where(slot == i, holder_ref[i], held)
    route = route_ref[...]
    share = route / jnp.sum(route, axis=0, keepdims=True)
    per_slot = jnp.zeros((extra, rows), jnp.float32)
    for k in range(ids_ref.shape[0]):
        per_slot += jnp.where(ids_ref[k : k + 1] == held, share[k : k + 1], 0.0)
    high = per_slot.astype(jnp.bfloat16).astype(jnp.float32)
    both = jnp.where(part < experts, high, jnp.where(part < 2 * experts, per_slot - high, 0.0))
    same = lax.broadcasted_iota(jnp.int32, (rows, rows), 0) == lax.broadcasted_iota(
        jnp.int32, (rows, rows), 1
    )
    turned = lax.dot_general(
        same.astype(jnp.bfloat16),
        both.astype(jnp.bfloat16),
        (((1,), (1,)), ((), ())),
        preferred_element_type=jnp.float32,
    )
    meta = turned.astype(jnp.bfloat16)
    out_ref[:, width:] = meta
    meta_ref[...] = meta
    choose(count, slot_ref, out_ref, meta, outs)
    clear(outs, count, width)


def packed_shape(count, width):
    full, _, columns = packing(count, width)
    return jax.ShapeDtypeStruct((full, width + columns), jnp.bfloat16)


def make_payload(slot, tokens, norm_gain, expert_ids, route_weight, holder, count):
    rows, width = tokens.shape
    experts = holder.shape[0]
    extra = -(-2 * experts // LANES) * LANES
    vmem = pl.BlockSpec(memory_space=pltpu.VMEM)
    outs = pl.pallas_call(
        functools.partial(payload_kernel, experts, count),
        out_shape=[
            jax.ShapeDtypeStruct((rows, width + extra), jnp.bfloat16),
            jax.ShapeDtypeStruct((rows, extra), jnp.bfloat16),
        ]
        + [packed_shape(count, width)] * PLANE,
        in_specs=[pl.BlockSpec(memory_space=pltpu.SMEM)] * 2 + [vmem] * 4,
        out_specs=[vmem] * (PLANE + 2),
        compiler_params=pltpu.CompilerParams(vmem_limit_bytes=LARGE),
        name="payload",
    )(slot, holder, tokens, norm_gain.reshape(1, -1), expert_ids.T, route_weight.T)
    return outs[0], outs[1], outs[2:]


def dispatch_kernel(count, slot_ref, base_ref, *outs):
    width = base_ref.shape[1] // CHUNK * CHUNK
    choose(count, slot_ref, base_ref, base_ref[:, width:], outs)
    clear(outs, count, width)


def raw_dispatch_kernel(count, slot_ref, tokens_ref, meta_ref, gain_ref, *refs):
    outs, rows_buf = refs[:PLANE], refs[PLANE]
    rows_buf[...] = normed(tokens_ref, gain_ref)
    choose(count, slot_ref, rows_buf, meta_ref[...], outs)
    clear(outs, count, tokens_ref.shape[1])


def dispatch(slot, base, count, width):
    vmem = pl.BlockSpec(memory_space=pltpu.VMEM)
    raw = isinstance(base, tuple)
    operands = base if raw else (base,)
    tokens = operands[0].shape[0]
    return pl.pallas_call(
        functools.partial(raw_dispatch_kernel if raw else dispatch_kernel, count),
        out_shape=[packed_shape(count, width)] * PLANE,
        in_specs=[pl.BlockSpec(memory_space=pltpu.SMEM)] + [vmem] * len(operands),
        out_specs=[vmem] * PLANE,
        scratch_shapes=[pltpu.VMEM((tokens, width), jnp.bfloat16)] if raw else [],
        cost_estimate=pl.CostEstimate(
            flops=2 * PLANE * count * tokens * width,
            bytes_accessed=2 * (tokens + PLANE * count) * width,
            transcendentals=0,
        ),
        compiler_params=pltpu.CompilerParams(vmem_limit_bytes=SMALL),
        name="dispatch",
    )(slot, *operands)


def combine_kernel(extras, experts, count, slot_ref, meta_ref, *refs):
    results, terms, out_ref = refs[:PLANE], refs[PLANE : PLANE + extras], refs[-1]
    tokens, extra = meta_ref.shape
    width = out_ref.shape[1]
    size = padded_rows(count)
    row = lax.broadcasted_iota(jnp.int32, (tokens, tokens), 0)
    column = lax.broadcasted_iota(jnp.int32, (tokens, tokens), 1)
    lane = lax.broadcasted_iota(jnp.int32, (tokens, extra), 1)
    meta = meta_ref[...].astype(jnp.float32)
    before = (column < row).astype(jnp.bfloat16)
    target = lax.broadcasted_iota(jnp.int32, (tokens, size), 1)
    chooser, shares = [], []
    for j in range(PLANE):
        at_slot = lane == (slot_ref[0] ^ j)
        high = jnp.sum(jnp.where(at_slot, meta, 0.0), axis=1, keepdims=True)
        routed = high > 0.0
        ones = jnp.broadcast_to(jnp.where(routed, 1.0, 0.0), (tokens, size)).astype(jnp.bfloat16)
        place = jnp.dot(before, ones, preferred_element_type=jnp.float32)
        mine = jnp.where((target == place.astype(jnp.int32)) & routed, 1.0, 0.0)
        mine = mine.astype(jnp.bfloat16)
        both = jnp.where(at_slot | (lane == (slot_ref[0] ^ j) + experts), meta, 0.0)
        per_row = lax.dot_general(
            mine,
            both.astype(jnp.bfloat16),
            (((0,), (0,)), ((), ())),
            preferred_element_type=jnp.float32,
        )
        shares.append(jnp.sum(per_row, axis=1, keepdims=True))
        chooser.append(mine)
    chooser = jnp.concatenate(chooser, 1)
    shares = jnp.concatenate(shares, 0)
    for at in chunks(width):
        rows = jnp.concatenate([unpack(r, at, count, width) for r in results], 0)
        rows = (rows * shares).astype(jnp.bfloat16)
        total = jnp.dot(chooser, rows, preferred_element_type=jnp.float32)
        if terms:
            part, start = divmod(at.start, width // len(terms))
            total = total + terms[part][:, start : start + CHUNK].astype(jnp.float32)
        out_ref[:, at] = total.astype(out_ref.dtype)


def combine(slot, base, results, terms, dtype, experts, count, width):
    tokens, padded = base.shape
    extra = padded % CHUNK
    whole = lambda a: pl.BlockSpec(a.shape, lambda i: (0, 0))
    return pl.pallas_call(
        functools.partial(combine_kernel, len(terms), experts, count),
        grid=(1,),
        out_shape=jax.ShapeDtypeStruct((tokens, width), dtype),
        in_specs=[
            pl.BlockSpec(memory_space=pltpu.SMEM),
            pl.BlockSpec((tokens, extra), lambda i: (0, padded // extra - 1)),
        ]
        + [whole(a) for a in (*results, *terms)],
        out_specs=pl.BlockSpec((tokens, width), lambda i: (0, 0)),
        cost_estimate=pl.CostEstimate(
            flops=2 * PLANE * count * tokens * width,
            bytes_accessed=2 * (tokens + PLANE * count) * width,
            transcendentals=0,
        ),
        compiler_params=pltpu.CompilerParams(vmem_limit_bytes=SMALL),
        name="combine",
    )(slot, base, *results, *terms)


def ffn_kernel(count, *refs):
    blocks, refs = refs[:PLANE], refs[PLANE:]
    gate_m, up_m, down_m, gate_p, up_p, down_p = refs[:6]
    outs, (rows_buf, hid_buf) = refs[6 : 6 + PLANE], refs[6 + PLANE :]
    width, half = gate_m.shape
    size = padded_rows(count)
    for at in chunks(width):
        for i, block in enumerate(blocks):
            rows = unpack(block, at, count, width)
            rows_buf[i * size : (i + 1) * size, at] = rows.astype(jnp.bfloat16)
    for side, (gate_w, up_w) in enumerate(((gate_m, up_m), (gate_p, up_p))):
        gate = jnp.dot(rows_buf[...], gate_w[...], preferred_element_type=jnp.float32)
        up = jnp.dot(rows_buf[...], up_w[...], preferred_element_type=jnp.float32)
        hid_buf[:, side * half : (side + 1) * half] = (
            gate / (1.0 + jnp.exp(-gate)) * up
        ).astype(jnp.bfloat16)
    for at in chunks(width):
        result = jnp.dot(hid_buf[:, :half], down_m[:, at], preferred_element_type=jnp.float32)
        result += jnp.dot(hid_buf[:, half:], down_p[:, at], preferred_element_type=jnp.float32)
        for i in range(PLANE):
            pack(outs[i], result[i * size : (i + 1) * size], at, count, width)
    clear(outs, count, width)


def run_ffn(blocks, weights, count):
    rows = PLANE * padded_rows(count)
    width, half = weights[0].shape
    vmem = pl.BlockSpec(memory_space=pltpu.VMEM)
    return pl.pallas_call(
        functools.partial(ffn_kernel, count),
        out_shape=[packed_shape(count, width)] * PLANE,
        in_specs=[vmem] * (PLANE + 6),
        out_specs=[vmem] * PLANE,
        scratch_shapes=[
            pltpu.VMEM((rows, width), jnp.bfloat16),
            pltpu.VMEM((rows, 2 * half), jnp.bfloat16),
        ],
        compiler_params=pltpu.CompilerParams(vmem_limit_bytes=SMALL),
        cost_estimate=pl.CostEstimate(
            flops=2 * rows * width * half * 6,
            bytes_accessed=12 * width * half + 4 * rows * width,
            transcendentals=rows * half * 2,
        ),
        name="ffn",
    )(*blocks, *weights)


def local(
    tokens,
    queries,
    keys_local,
    values_local,
    prompt_keys,
    prompt_values,
    norm_gain,
    expert_ids,
    route_weight,
    stored_gate,
    stored_up,
    stored_down,
    holder,
):
    owners = lax.axis_size("expert")
    experts = holder.shape[0]
    columns = owners // 4
    f32, bf16 = jnp.float32, jnp.bfloat16

    def swap(value, offset):
        return lax.ppermute(value, "expert", [(i, i ^ offset) for i in range(owners)])

    def partner(value):
        return lax.ppermute(value, "dp", [(0, 1), (1, 0)])

    own_weights = (stored_gate[0], stored_up[0], stored_down[0])
    weights = own_weights + tuple(partner(w) for w in own_weights)
    slot = lax.axis_index("expert").astype(jnp.int32).reshape(1)
    width = tokens.shape[1]
    count = capacity(tokens.shape[0], owners)
    payload, meta, chosen = make_payload(
        slot, tokens, norm_gain, expert_ids, route_weight, holder, count
    )
    bases, blocks, outs = {}, {}, {}

    def gather(k, base, ready=None):
        bases[k] = base
        if ready is None:
            ready = dispatch(slot, base, count, width)
        own, to_x, to_y, to_d = ready
        blocks[k] = (own, swap(to_x, 1), swap(to_y, 2), swap(to_d, 3))

    def serve(k):
        own, to_x, to_y, to_d = run_ffn(blocks[k], weights, count)
        outs[k] = (own, swap(to_x, 1), swap(to_y, 2), swap(to_d, 3))

    def collect(k, terms=(), dtype=bf16):
        return combine(slot, bases[k], outs[k], terms, dtype, experts, count, width)

    gather(0, payload, chosen)
    result = []
    for part in range(KVH):
        result.append(
            attend(
                part, tokens, queries, keys_local, values_local, prompt_keys, prompt_values
            )
        )
    for first in range(0, columns, 4):
        if first == 0:
            lanes = swap(meta, 4)
            gather(1, (swap(tokens, 4), lanes, norm_gain.reshape(1, -1)))
            bases[1] = lanes
            gather(3, swap(payload, 12))
            gather(2, swap(bases[3], 4))
        else:
            gather(first, swap(payload, 4 * first))
            gather(first + 1, swap(payload, 4 * first + 4))
            gather(first + 2, swap(payload, 4 * first + 8))
            gather(first + 3, swap(bases[first + 2], 4))
    for k in range(columns):
        serve(k)
    sums = []
    for first in range(0, columns, 4):
        passed = swap(collect(first + 3), 4)
        sums.append(swap(collect(first + 2, (passed,)), 4 * first + 8))
        sums.append(swap(collect(first + 1), 4 * first + 4))
        if first:
            sums.append(swap(collect(first), 4 * first))
    result = collect(0, result, f32)
    for part in sums:
        result = result + part.astype(f32)
    return result.astype(bf16)


def solution(mesh):
    return jax.shard_map(
        local,
        mesh=mesh,
        in_specs=(
            P(("group", "expert", "dp"), None),
            P(("group", "expert", "dp"), None),
            P(("group", "expert", "dp"), None),
            P(("group", "expert", "dp"), None),
            P("group", None),
            P("group", None),
            P(),
            P(("group", "expert", "dp"), None),
            P(("group", "expert", "dp"), None),
            P("expert", None, "dp"),
            P("expert", None, "dp"),
            P("expert", "dp", None),
            P(),
        ),
        out_specs=P(("group", "expert", "dp"), None),
        check_vma=False,
    )
```
